512 devices in a mesh: dp: 32 (over y_hi, z, core), expert: 16 (over x, y_lo).
Axes of the slice: x: 4, y: 8 (y_hi: 2, y_lo: 4; y = y_hi * 4 + y_lo), z: 8, core: 2. Of those that a mesh axis runs over, the one named last changes fastest.
Arguments:
- tokens: bfloat16 [2048, 4096], P('expert', 'dp'), may hold values from -6 to 6
- cotangent: bfloat16 [2048, 4096], P('expert', 'dp'), may hold values from -1.125 to 1.125
- routes: int32 [2048, 2], P('expert'), may hold values from 0 to 15, all different within a row; in each aligned block of 128 rows (0 to 127, 128 to 255, ...) at most 40 rows name the same one
- gates: float32 [2048, 2], P('expert'), may hold values from 0.05 to 1
- expert_weights: bfloat16 [16, 3, 2048, 4096], P('expert', None, 'dp'), may hold values from -0.09375 to 0.09375
Outputs:
- weight_grads: bfloat16 [16, 3, 2048, 4096], P('expert', None, 'dp')
The draws below stay inside these ranges and needn't reach their ends.
Inputs may be any that keep to these rules, and one draw needn't show every extreme that they name: Each row names 2 different experts; within the 128 rows of one index of the expert axis no expert is named by more than 40 routes.
All inputs are finite; a program needn't handle non-finite values.
Results may differ from the reference program's by a relative error of at most 0.0057.
Values may be sent and summed in bfloat16 or wider, within the bound.
No kernel may reach another device: no remote copies, remote signals or barrier semaphores. Data moves between devices by JAX's collectives and lax.ppermute only.
A program may use at most 64 MiB of HBM per device.

```python
import math
import jax
import jax.numpy as jnp
import numpy as np
from jax import lax

D = 4096
FH = 2048
E = 16
KG = 2
TOK_DEV = 128
CAP = 40
TOKENS = 2048
ROWS_E = 256


def levels(rng, dims, shards, smallest, top_value):
    def one(dim, blocks):
        steps = jax.random.uniform(jax.random.fold_in(jax.random.fold_in(rng, 6), dim), (blocks,), jnp.float32, smallest / len(shards), top_value / len(shards))
        return jnp.repeat(jnp.exp(steps), dims[dim] // blocks).reshape((-1,) + (1,) * (len(dims) - dim - 1))

    loudness = one(*shards[0])
    for cut in shards[1:]:
        loudness = loudness * one(*cut)
    return loudness


def deal_out(stream_key, own, number, rows, count, top, bound, lean):
    ranking = jax.random.permutation(stream_key, count)
    heavy_load, ordinary = portions_of(count, rows * top, bound, lean, True), portions_of(count, rows * top, bound, lean, False)
    places = jnp.arange(count)

    def named(sizes, offset_by):
        used = int((sizes > 0).sum())
        fixed = max(1, used // 4)
        shifted = fixed + (places - fixed + offset_by * (used - fixed)) % max(1, count - fixed)
        return jnp.zeros((count,), jnp.int32).at[ranking[jnp.where(places < fixed, places, shifted)]].set(jnp.asarray(sizes, jnp.int32))

    sizes = jnp.where(number % 4 == 0, named(heavy_load, number // 4), named(ordinary, number - number // 4 - 1))
    mixed = jax.random.permutation(jax.random.fold_in(own, 3), count)
    giver, sink = mixed[0:count // 2 * 2:2], mixed[1:count // 2 * 2:2]
    room = jnp.minimum(sizes[giver] - 1, bound - sizes[sink]) // 2
    room = jnp.where((giver == ranking[0]) | (sink == ranking[0]) | (sizes[sink] == 0), 0, jnp.maximum(room, 0))
    shifted = jax.random.randint(jax.random.fold_in(own, 4), (count // 2,), 0, 1 << 20) % (room + 1)
    sizes = sizes.at[giver].add(-shifted).at[sink].add(shifted)
    members = jnp.searchsorted(jnp.cumsum(sizes), jnp.arange(rows * top), side="right").astype(jnp.int32)
    table = members.reshape(top, rows).T
    table = table[jax.random.permutation(jax.random.fold_in(own, 1), rows)]
    offset_by = jax.random.randint(jax.random.fold_in(own, 2), (rows, 1), 0, top)
    return jnp.take_along_axis(table, (jnp.arange(top)[None, :] + offset_by) % top, axis=1)


def portions_of(amount, total, bound, lean, full):
    loads = [(1 << 20) // math.isqrt(standing ** lean) + 1 for standing in range(1, amount + 1)]
    largest = bound if full else min(bound, max(-(-total // amount), total * loads[0] // sum(loads)))
    least = 1 if total - largest >= amount - 1 else 0
    holding, surplus = [largest] + [least] * (amount - 1), total - largest - least * (amount - 1)
    while surplus > 0:
        movable = [i for i in range(1, amount) if holding[i] < largest] or [i for i in range(1, amount) if holding[i] < bound]
        mass, left = sum([loads[i] for i in movable]), surplus
        for i in movable:
            extra = min(bound - holding[i], max(1, left * loads[i] // mass), surplus)
            holding[i] = holding[i] + extra
            surplus = surplus - extra
    return np.array(holding)


def normal_values(stream_key, shape, width, limit, split=(), kind=jnp.bfloat16):
    entries = width * jax.random.normal(stream_key, shape, jnp.float32)
    if split:
        entries = entries * levels(stream_key, shape, split, -0.22, 0.18)
    return jnp.clip(entries, -limit, limit).astype(kind)


def setup_inputs(seed: int = 0) -> dict:
    streams_of = jax.random.split(jax.random.key(seed), 6)
    tokens = normal_values(streams_of[0], (TOKENS, D), 1.0, 6.0, ((0, 16), (1, 32)))
    cotangent = normal_values(streams_of[1], (TOKENS, D), (3.0 * ROWS_E ** -0.5), 1.125, ((0, 16), (1, 32)))
    routes_keys = jax.random.split(jax.random.fold_in(streams_of[2], 1), TOKENS // TOK_DEV)
    routes_turns = jax.random.permutation(jax.random.fold_in(streams_of[2], 3), TOKENS // TOK_DEV)
    routes = jax.vmap(lambda own, number: deal_out(jax.random.fold_in(streams_of[2], 2), own, number, TOK_DEV, E, KG, CAP, 2))(routes_keys, routes_turns).reshape((TOKENS, KG))
    gates = jnp.clip(jnp.exp(math.log(1.0) - 2.9957323 * jax.random.uniform(streams_of[3], (TOKENS, KG), jnp.float32) ** levels(streams_of[3], (TOKENS, KG), ((0, 16),), -0.2, 0.2)), 0.05, 1.0)
    expert_weights = normal_values(streams_of[4], (E, 3, FH, D), D ** -0.5, 0.09375, ((0, 16), (2, 32)))
    return {"tokens": tokens, "cotangent": cotangent, "routes": routes, "gates": gates, "expert_weights": expert_weights}


def row_terms(input_rows, scaled, weights):
    ins = input_rows.astype(jnp.float32)
    outs = scaled.astype(jnp.float32)
    gate_part = jnp.dot(input_rows, weights[0].T, preferred_element_type=jnp.float32)
    up_part = jnp.dot(input_rows, weights[1].T, preferred_element_type=jnp.float32)
    sigmoid_part = jax.nn.sigmoid(gate_part)
    hidden = (gate_part * sigmoid_part * up_part).astype(jnp.bfloat16)
    back_hidden = jnp.dot(scaled, weights[2].T, preferred_element_type=jnp.float32)
    derivative = sigmoid_part * (1.0 + gate_part * (1.0 - sigmoid_part))
    pre_gate = (back_hidden * up_part * derivative).astype(jnp.bfloat16)
    pre_up = (back_hidden * gate_part * sigmoid_part).astype(jnp.bfloat16)
    gate_grads = jnp.dot(pre_gate.T, input_rows, preferred_element_type=jnp.float32)
    up_grads = jnp.dot(pre_up.T, input_rows, preferred_element_type=jnp.float32)
    down_grads = jnp.dot(hidden.T, scaled, preferred_element_type=jnp.float32)
    return jnp.stack([gate_grads, up_grads, down_grads], axis=0)


def reference(tokens, cotangent, routes, gates, expert_weights):
    block_rows = 128
    expert_total = expert_weights.shape[0]
    per_token = routes.shape[1]
    routed = routes.reshape(-1).astype(jnp.int32)
    route_total = routed.shape[0]
    sorted_order = jnp.argsort(routed, stable=True).astype(jnp.int32)
    picked = routed[sorted_order]
    matches = (routed[:, None] == jnp.arange(expert_total, dtype=jnp.int32)[None, :]).astype(jnp.int32)
    counts = jnp.sum(matches, axis=0)
    starts = jnp.cumsum(counts) - counts
    padded = (counts + block_rows - 1) // block_rows * block_rows
    limits = jnp.cumsum(padded)
    block_starts = limits - padded
    position = jnp.arange(route_total, dtype=jnp.int32) - starts[picked]
    destination = block_starts[picked] + position
    slot_total = ((route_total + block_rows - 1) // block_rows + expert_total) * block_rows
    source = jnp.full((slot_total,), route_total, jnp.int32).at[destination].set(sorted_order)
    blocks = slot_total // block_rows
    block_first = jnp.arange(blocks, dtype=jnp.int32) * block_rows
    block_expert = jnp.minimum(jnp.sum((limits[None, :] <= block_first[:, None]).astype(jnp.int32), axis=1), expert_total - 1)
    gates_flat = gates.reshape(-1)

    def one_block(running_sum, item):
        index_rows, expert = item
        filled = index_rows < route_total
        clamped = jnp.minimum(index_rows, route_total - 1)
        token_index = clamped // per_token
        input_rows = jnp.where(filled[:, None], tokens[token_index], jnp.zeros((), tokens.dtype))
        weight = jnp.where(filled, gates_flat[clamped], jnp.zeros((), gates_flat.dtype))
        scaled = (weight[:, None] * cotangent[token_index].astype(jnp.float32)).astype(jnp.bfloat16)
        block_term = row_terms(input_rows, scaled, expert_weights[expert])
        return running_sum.at[expert].add(block_term), None

    start_sum = jnp.zeros(expert_weights.shape, jnp.float32)
    final_sum, unused = lax.scan(one_block, start_sum, (source.reshape(blocks, block_rows), block_expert))
    return final_sum.astype(jnp.bfloat16)
```

```python
import jax
import jax.numpy as jnp
from jax import lax
from jax.experimental import pallas as pl
from jax.experimental.pallas import tpu as pltpu
from jax.sharding import PartitionSpec as P

CAP = 40
BF16 = jnp.bfloat16
F32 = jnp.float32


def dp_index(half, ring, core, ring_size):
    return (half * ring_size + ring) * 2 + core


def ring_pairs(step, ring_size):
    return [
        (dp_index(h, z, c, ring_size), dp_index(h, (z + step) % ring_size, c, ring_size))
        for h in range(2)
        for z in range(ring_size)
        for c in range(2)
    ]


def route_kernel(routes_ref, gates_ref, select_ref, weight_ref):
    tokens, experts = routes_ref.shape[0], select_ref.shape[0] // CAP
    lanes = lax.broadcasted_iota(jnp.int32, (tokens, experts), 1)
    named = jnp.zeros((tokens, experts), F32)
    weight = jnp.zeros((tokens, experts), F32)
    for k in range(routes_ref.shape[1]):
        hit = routes_ref[:, k : k + 1] == lanes
        named = named + jnp.where(hit, 1.0, 0.0)
        weight = weight + jnp.where(hit, gates_ref[:, k : k + 1], 0.0)
    down = lax.broadcasted_iota(jnp.int32, (tokens, tokens), 0)
    across = lax.broadcasted_iota(jnp.int32, (tokens, tokens), 1)
    before = jnp.where(down < across, 1.0, 0.0).astype(BF16)
    earlier = lax.dot_general(
        named.astype(BF16), before, (((0,), (0,)), ((), ())), preferred_element_type=F32
    )
    named_across = named.T
    weight_across = weight.T
    place = jnp.where(named_across > 0.0, earlier, -1.0)
    slots = lax.broadcasted_iota(jnp.int32, (CAP, tokens), 0).astype(F32)
    for e in range(experts):
        hit = place[e : e + 1, :] == slots
        select_ref[e * CAP : (e + 1) * CAP, :] = jnp.where(hit, 1.0, 0.0).astype(BF16)
        gate = jnp.sum(jnp.where(hit, weight_across[e : e + 1, :], 0.0), axis=1, keepdims=True)
        weight_ref[e * CAP : (e + 1) * CAP, :] = jnp.broadcast_to(
            gate, (CAP, weight_ref.shape[1])
        )


def pack_kernel(select_ref, weight_ref, own_ref, other_ref, out_ref):
    width = own_ref.shape[1] // 2
    select = select_ref[...]
    weight = weight_ref[...]
    for j, ref in enumerate((own_ref, other_ref)):
        rows = jnp.dot(select, ref[...], preferred_element_type=F32)
        out_ref[:, j * width : (j + 1) * width] = rows[:, :width].astype(BF16)
        out_ref[:, (2 + j) * width : (3 + j) * width] = (rows[:, width:] * weight).astype(BF16)


def grads_kernel(ring_size, parts, index_ref, weights_ref, *refs):
    count = sum(len(p) for p in parts)
    sources, out_ref = refs[:count], refs[count]
    rows_buf, weights_buf, total, sems, weight_sem = refs[count + 1 :]
    blocks, rows, width = rows_buf.shape
    half = width // 4
    fetch_weights = pltpu.make_async_copy(weights_ref, weights_buf, weight_sem)
    fetch_weights.start()
    copies = []
    at = 0
    for k, part in enumerate(parts):
        mine = []
        for first, size in part:
            copy = pltpu.make_async_copy(
                sources[at], rows_buf.at[k, pl.ds(first, size)], sems.at[at]
            )
            copy.start()
            mine.append(copy)
            at += 1
        copies.append(mine)
    fetch_weights.wait()
    hidden_units = weights_buf.shape[2]
    me = index_ref[0]
    core = lax.rem(me, 2)
    ring = lax.rem(me // 2, ring_size)
    side = me // (2 * ring_size)

    def offset(k, j):
        step, swapped = k // 2, lax.rem(k, 2)
        z = lax.rem(ring - step + ring_size, ring_size)
        h = side + j - 2 * side * j
        c = core + swapped - 2 * core * swapped
        return pl.multiple_of(((h * ring_size + z) * 2 + c) * half, half)

    along = (((1,), (1,)), ((), ()))

    def weight_block(m, k):
        return jnp.concatenate(
            [weights_buf[0, m, :, pl.ds(offset(k, j), half)] for j in range(2)], axis=1
        )

    total[...] = jnp.zeros_like(total)
    for k in range(blocks):
        for copy in copies[k]:
            copy.wait()
        pair = jnp.concatenate([weight_block(0, k), weight_block(1, k)], axis=0)
        total[:, : 2 * hidden_units] += lax.dot_general(
            rows_buf[k, :, : 2 * half], pair, along, preferred_element_type=F32
        )
        total[:, 2 * hidden_units :] += lax.dot_general(
            rows_buf[k, :, 2 * half :], weight_block(2, k), along, preferred_element_type=F32
        )
    gate_part = total[:, :hidden_units]
    up_part = total[:, hidden_units : 2 * hidden_units]
    back_hidden = total[:, 2 * hidden_units :]
    sigmoid_part = jax.nn.sigmoid(gate_part)
    silu = gate_part * sigmoid_part
    hidden = (silu * up_part).astype(BF16)
    derivative = sigmoid_part * (1.0 + gate_part * (1.0 - sigmoid_part))
    pre_gate = (back_hidden * up_part * derivative).astype(BF16)
    pre_up = (back_hidden * silu).astype(BF16)
    both = jnp.concatenate([pre_gate, pre_up], axis=1).T
    hidden_t = hidden.T

    def one_block(k, carry):
        ins = jnp.dot(both, rows_buf[k, :, : 2 * half], preferred_element_type=F32).astype(BF16)
        outs = jnp.dot(hidden_t, rows_buf[k, :, 2 * half :], preferred_element_type=F32).astype(BF16)
        for j in range(2):
            cols = pl.ds(offset(k, j), half)
            cut = slice(j * half, (j + 1) * half)
            out_ref[0, 0, :, cols] = ins[:hidden_units, cut]
            out_ref[0, 1, :, cols] = ins[hidden_units:, cut]
            out_ref[0, 2, :, cols] = outs[:, cut]
        return carry

    lax.fori_loop(0, blocks, one_block, 0)


def per_device(tokens, cotangent, routes, gates, expert_weights):
    groups = lax.axis_size("expert")
    ring_size = lax.axis_size("dp") // 4
    slots = groups * CAP
    rows, width = tokens.shape
    own = jnp.concatenate([tokens, cotangent], axis=1)
    other = lax.ppermute(own, "dp", [(i, (i + 2 * ring_size) % (4 * ring_size)) for i in range(4 * ring_size)])
    select, weight = pl.pallas_call(
        route_kernel,
        out_shape=(
            jax.ShapeDtypeStruct((slots, rows), BF16),
            jax.ShapeDtypeStruct((slots, width), F32),
        ),
    )(routes, gates)
    send = pl.pallas_call(
        pack_kernel, out_shape=jax.ShapeDtypeStruct((slots, 4 * width), BF16)
    )(select, weight, own, other)
    mine = lax.all_to_all(
        send.reshape(groups, CAP, 4 * width), "expert", split_axis=0, concat_axis=0, tiled=True
    ).reshape(slots, 4 * width)

    right, left = ring_pairs(1, ring_size), ring_pairs(-1, ring_size)
    swap = [(i, i ^ 1) for i in range(4 * ring_size)]

    def swapped(x):
        return lax.ppermute(x, "dp", swap)

    held = {0: [mine]}
    from_left, from_right = mine, mine
    half_ring = ring_size // 2
    for step in range(1, half_ring):
        from_left = lax.ppermute(from_left, "dp", right)
        from_right = lax.ppermute(from_right, "dp", left)
        held[step] = [from_left]
        held[ring_size - step] = [from_right]
    cut = slots // 2
    held[half_ring] = [
        lax.ppermute(from_left[:cut], "dp", right),
        lax.ppermute(from_right[cut:], "dp", left),
    ]
    sources, parts = [], []
    for step in range(ring_size):
        pieces = held[step]
        spans, first = [], 0
        for piece in pieces:
            spans.append((first, piece.shape[0]))
            first += piece.shape[0]
        for group in (pieces, [swapped(p) for p in pieces]):
            sources.extend(group)
            parts.append(tuple(spans))
    me = lax.axis_index("dp").astype(jnp.int32).reshape(1)
    blocks = 2 * ring_size
    hidden_units = expert_weights.shape[2]
    any_spec = pl.BlockSpec(memory_space=pl.ANY)
    return pl.pallas_call(
        lambda *refs: grads_kernel(ring_size, parts, *refs),
        out_shape=jax.ShapeDtypeStruct(expert_weights.shape, BF16),
        in_specs=[pl.BlockSpec(memory_space=pltpu.SMEM), any_spec] + [any_spec] * len(sources),
        out_specs=pl.BlockSpec(memory_space=pltpu.VMEM),
        scratch_shapes=[
            pltpu.VMEM((blocks, slots, 4 * width), BF16),
            pltpu.VMEM(expert_weights.shape, BF16),
            pltpu.VMEM((slots, 3 * hidden_units), F32),
            pltpu.SemaphoreType.DMA((len(sources),)),
            pltpu.SemaphoreType.DMA,
        ],
        compiler_params=pltpu.CompilerParams(vmem_limit_bytes=40 << 20),
    )(me, expert_weights, *sources)


def solution(mesh):
    return jax.shard_map(
        per_device,
        mesh=mesh,
        in_specs=(
            P("expert", "dp"),
            P("expert", "dp"),
            P("expert", None),
            P("expert", None),
            P("expert", None, "dp", None),
        ),
        out_specs=P("expert", None, "dp", None),
        check_vma=False,
    )
```

```python
import jax
import jax.numpy as jnp
from jax import lax
from jax.experimental import pallas as pl
from jax.experimental.pallas import tpu as pltpu
from jax.sharding import Mesh
from jax.sharding import PartitionSpec as P

CAP = 40
BF16 = jnp.bfloat16
F32 = jnp.float32


def pack_kernel(routes_ref, gates_ref, tokens_ref, cotangent_ref, rows_ref, scaled_ref):
    tokens = routes_ref.shape[0]
    copies, slots = rows_ref.shape[0], rows_ref.shape[1]
    experts = slots // CAP
    lanes = lax.broadcasted_iota(jnp.int32, (tokens, experts), 1)
    named = jnp.zeros((tokens, experts), F32)
    weight = jnp.zeros((tokens, experts), F32)
    for k in range(routes_ref.shape[1]):
        hit = routes_ref[:, k : k + 1] == lanes
        named = named + jnp.where(hit, 1.0, 0.0)
        weight = weight + jnp.where(hit, gates_ref[:, k : k + 1], 0.0)
    down = lax.broadcasted_iota(jnp.int32, (tokens, tokens), 0)
    across = lax.broadcasted_iota(jnp.int32, (tokens, tokens), 1)
    before = jnp.where(down < across, 1.0, 0.0).astype(BF16)
    earlier = lax.dot_general(
        named.astype(BF16), before, (((0,), (0,)), ((), ())), preferred_element_type=F32
    )
    named_across = named.T
    weight_across = weight.T
    place = jnp.where(named_across > 0.0, earlier, -1.0)
    places = lax.broadcasted_iota(jnp.int32, (CAP, tokens), 0).astype(F32)
    select, weights = [], []
    for e in range(experts):
        hit = place[e : e + 1, :] == places
        select.append(jnp.where(hit, 1.0, 0.0))
        weights.append(
            jnp.sum(jnp.where(hit, weight_across[e : e + 1, :], 0.0), axis=1, keepdims=True)
        )
    select = jnp.concatenate(select, axis=0).astype(BF16)
    weights = jnp.concatenate(weights, axis=0)
    rows = jnp.dot(select, tokens_ref[...], preferred_element_type=F32).astype(BF16)
    scaled = jnp.dot(select, cotangent_ref[...], preferred_element_type=F32)
    scaled = (scaled * weights).astype(BF16)
    for j in range(copies):
        rows_ref[j] = rows
        scaled_ref[j] = scaled


def grads_kernel(ring_size, parts, index_ref, weights_ref, *refs):
    count = 2 * len(parts)
    sources, out_ref = refs[:count], refs[count]
    rows_buf, scaled_buf, weights_buf, total, sems, weight_sem = refs[count + 1 :]
    blocks, halves, slots, half = rows_buf.shape
    fetch_weights = pltpu.make_async_copy(weights_ref, weights_buf, weight_sem)
    fetch_weights.start()
    copies = []
    for n, (first, size) in enumerate(parts):
        pair = []
        for m, buf in enumerate((rows_buf, scaled_buf)):
            copy = pltpu.make_async_copy(
                sources[2 * n + m], buf.at[pl.ds(first, size)], sems.at[2 * n + m]
            )
            copy.start()
            pair.append(copy)
        copies.append(pair)
    fetch_weights.wait()
    hidden_units = weights_buf.shape[2]
    ring, core = index_ref[0], index_ref[1]
    far = ring_size // 2

    def offset(b, j):
        t, i = b // 2, lax.rem(b, 2)
        turned = jnp.where(t >= far, 1, 0)
        step = jnp.where(t == ring_size - 1, far, t - turned * (far - 1))
        flip = jnp.where(t == ring_size - 1, 0, turned)
        way = (1 - 2 * core) * (1 - 2 * turned)
        z = lax.rem(ring - way * step + 2 * ring_size, ring_size)
        other = lax.rem(flip + i, 2)
        c = core + other - 2 * core * other
        return pl.multiple_of(((j * ring_size + z) * 2 + c) * half, half)

    along = (((1,), (1,)), ((), ()))

    def weight_block(m, b):
        return jnp.concatenate(
            [weights_buf[0, m, :, pl.ds(offset(b, j), half)] for j in range(halves)], axis=1
        )

    def block(buf, b):
        return jnp.concatenate([buf[b, j] for j in range(halves)], axis=1)

    total[...] = jnp.zeros_like(total)
    for n, (first, size) in enumerate(parts):
        for copy in copies[n]:
            copy.wait()
        for b in range(first, first + size):
            pair = jnp.concatenate([weight_block(0, b), weight_block(1, b)], axis=0)
            total[:, : 2 * hidden_units] += lax.dot_general(
                block(rows_buf, b), pair, along, preferred_element_type=F32
            )
            total[:, 2 * hidden_units :] += lax.dot_general(
                block(scaled_buf, b), weight_block(2, b), along, preferred_element_type=F32
            )
    gate_part = total[:, :hidden_units]
    up_part = total[:, hidden_units : 2 * hidden_units]
    back_hidden = total[:, 2 * hidden_units :]
    sigmoid_part = jax.nn.sigmoid(gate_part)
    silu = gate_part * sigmoid_part
    hidden = (silu * up_part).astype(BF16)
    derivative = sigmoid_part * (1.0 + gate_part * (1.0 - sigmoid_part))
    pre_gate = (back_hidden * up_part * derivative).astype(BF16)
    pre_up = (back_hidden * silu).astype(BF16)
    both = jnp.concatenate([pre_gate, pre_up], axis=1).T
    hidden_t = hidden.T

    def one_block(b, carry):
        ins = jnp.dot(both, block(rows_buf, b), preferred_element_type=F32).astype(BF16)
        outs = jnp.dot(hidden_t, block(scaled_buf, b), preferred_element_type=F32).astype(BF16)
        for j in range(halves):
            cols = pl.ds(offset(b, j), half)
            cut = slice(j * half, (j + 1) * half)
            out_ref[0, 0, :, cols] = ins[:hidden_units, cut]
            out_ref[0, 1, :, cols] = ins[hidden_units:, cut]
            out_ref[0, 2, :, cols] = outs[:, cut]
        return carry

    lax.fori_loop(0, blocks, one_block, 0)


def per_device(tokens, cotangent, routes, gates, expert_weights):
    groups = lax.axis_size("expert")
    ring_size = lax.axis_size("ring")
    slots = groups * CAP
    width = tokens.shape[1]
    packed = jax.ShapeDtypeStruct((2, slots, width), BF16)
    send = pl.pallas_call(pack_kernel, out_shape=(packed, packed))(
        routes, gates, tokens, cotangent
    )
    around = [
        (z * 2 + c, ((z + 1 - 2 * c) % ring_size) * 2 + c)
        for z in range(ring_size)
        for c in range(2)
    ]

    def swapped(x):
        return lax.ppermute(x, "core", [(0, 1), (1, 0)])

    chains = []
    for x in send:
        own = lax.all_to_all(
            x.reshape(2 * groups, CAP, width),
            ("half", "expert"),
            split_axis=0,
            concat_axis=0,
            tiled=True,
        ).reshape(1, 2, slots, width)
        held = jnp.concatenate([own, swapped(own)], axis=0)
        near, turned = [held], []
        for step in range(1, ring_size // 2):
            held = lax.ppermute(held, ("ring", "core"), around)
            near.append(held)
            turned.append(swapped(held))
        last = lax.ppermute(held[:1], ("ring", "core"), around)
        chains.append(near + turned + [last, swapped(last)])
    sources, parts, first = [], [], 0
    for a, b in zip(*chains):
        sources += [a, b]
        parts.append((first, a.shape[0]))
        first += a.shape[0]
    index = jnp.stack([lax.axis_index("ring"), lax.axis_index("core")]).astype(jnp.int32)
    hidden_units = expert_weights.shape[2]
    any_spec = pl.BlockSpec(memory_space=pl.ANY)
    return pl.pallas_call(
        lambda *refs: grads_kernel(ring_size, parts, *refs),
        out_shape=jax.ShapeDtypeStruct(expert_weights.shape, BF16),
        in_specs=[pl.BlockSpec(memory_space=pltpu.SMEM), any_spec] + [any_spec] * len(sources),
        out_specs=pl.BlockSpec(memory_space=pltpu.VMEM),
        scratch_shapes=[
            pltpu.VMEM((first, 2, slots, width), BF16),
            pltpu.VMEM((first, 2, slots, width), BF16),
            pltpu.VMEM(expert_weights.shape, BF16),
            pltpu.VMEM((slots, 3 * hidden_units), F32),
            pltpu.SemaphoreType.DMA((len(sources),)),
            pltpu.SemaphoreType.DMA,
        ],
        compiler_params=pltpu.CompilerParams(vmem_limit_bytes=40 << 20),
    )(index, expert_weights, *sources)


def solution(mesh):
    sizes = dict(zip(mesh.axis_names, mesh.devices.shape))
    fine = Mesh(
        mesh.devices.reshape(2, sizes["dp"] // 4, 2, sizes["expert"]),
        ("half", "ring", "core", "expert"),
    )
    dp = ("half", "ring", "core")
    return jax.shard_map(
        per_device,
        mesh=fine,
        in_specs=(
            P("expert", dp),
            P("expert", dp),
            P("expert", None),
            P("expert", None),
            P("expert", None, dp, None),
        ),
        out_specs=P("expert", None, dp, None),
        check_vma=False,
    )
```

```python
import jax
import jax.numpy as jnp
from jax import lax
from jax.experimental import pallas as pl
from jax.experimental.pallas import tpu as pltpu
from jax.sharding import Mesh
from jax.sharding import PartitionSpec as P

CAP = 40
BF16 = jnp.bfloat16
F32 = jnp.float32


def pack_kernel(routes_ref, gates_ref, tokens_ref, cotangent_ref, out_ref):
    tokens = routes_ref.shape[1]
    copies, slots, width = out_ref.shape
    experts = slots // CAP
    ids = lax.broadcasted_iota(jnp.int32, (experts, tokens), 0)
    named = jnp.zeros((experts, tokens), F32)
    weight = jnp.zeros((experts, tokens), F32)
    for k in range(routes_ref.shape[0]):
        hit = routes_ref[k : k + 1, :] == ids
        named = named + jnp.where(hit, 1.0, 0.0)
        weight = weight + jnp.where(hit, gates_ref[k : k + 1, :], 0.0)
    down = lax.broadcasted_iota(jnp.int32, (tokens, tokens), 0)
    across = lax.broadcasted_iota(jnp.int32, (tokens, tokens), 1)
    before = jnp.where(down < across, 1.0, 0.0).astype(BF16)
    earlier = jnp.dot(named.astype(BF16), before, preferred_element_type=F32)
    place = jnp.where(named > 0.0, earlier, -1.0)
    places = lax.broadcasted_iota(jnp.int32, (CAP, tokens), 0).astype(F32)
    select, weights = [], []
    for e in range(experts):
        hit = place[e : e + 1, :] == places
        select.append(jnp.where(hit, 1.0, 0.0))
        weights.append(jnp.sum(jnp.where(hit, weight[e : e + 1, :], 0.0), axis=1, keepdims=True))
    select = jnp.concatenate(select, axis=0).astype(BF16)
    weights = jnp.concatenate(weights, axis=0)
    rows = jnp.dot(select, tokens_ref[...], preferred_element_type=F32).astype(BF16)
    scaled = jnp.dot(select, cotangent_ref[...], preferred_element_type=F32)
    scaled = (scaled * weights).astype(BF16)
    for j in range(copies):
        out_ref[j, :, : width // 2] = rows
        out_ref[j, :, width // 2 :] = scaled


def grads_kernel(ring_size, parts, index_ref, weights_ref, *refs):
    count = 2 * len(parts)
    sources, out_ref = refs[:count], refs[count]
    rows_buf, scaled_buf, weights_buf, total, sems, weight_sem = refs[count + 1 :]
    blocks, halves, slots, half = rows_buf.shape
    fetch_weights = pltpu.make_async_copy(weights_ref, weights_buf, weight_sem)
    fetch_weights.start()
    copies = []
    for n, (first, size) in enumerate(parts):
        pair = []
        for m, buf in enumerate((rows_buf, scaled_buf)):
            copy = pltpu.make_async_copy(
                sources[2 * n + m], buf.at[pl.ds(first, size)], sems.at[2 * n + m]
            )
            copy.start()
            pair.append(copy)
        copies.append(pair)
    fetch_weights.wait()
    hidden_units = weights_buf.shape[2]
    ring, core = index_ref[0], index_ref[1]
    far = ring_size // 2

    def offset(b, j):
        t, i = b // 2, lax.rem(b, 2)
        turned = jnp.where(t >= far, 1, 0)
        step = jnp.where(t == ring_size - 1, far, t - turned * (far - 1))
        flip = jnp.where(t == ring_size - 1, 0, turned)
        way = (1 - 2 * core) * (1 - 2 * turned)
        z = lax.rem(ring - way * step + 2 * ring_size, ring_size)
        other = lax.rem(flip + i, 2)
        c = core + other - 2 * core * other
        return pl.multiple_of(((j * ring_size + z) * 2 + c) * half, half)

    along = (((1,), (1,)), ((), ()))

    def weight_block(m, b):
        return jnp.concatenate(
            [weights_buf[0, m, :, pl.ds(offset(b, j), half)] for j in range(halves)], axis=1
        )

    def block(buf, b):
        return jnp.concatenate([buf[b, j] for j in range(halves)], axis=1)

    total[...] = jnp.zeros_like(total)
    for n, (first, size) in enumerate(parts):
        for copy in copies[n]:
            copy.wait()
        for b in range(first, first + size):
            pair = jnp.concatenate([weight_block(0, b), weight_block(1, b)], axis=0)
            total[:, : 2 * hidden_units] += lax.dot_general(
                block(rows_buf, b), pair, along, preferred_element_type=F32
            )
            total[:, 2 * hidden_units :] += lax.dot_general(
                block(scaled_buf, b), weight_block(2, b), along, preferred_element_type=F32
            )
    gate_part = total[:, :hidden_units]
    up_part = total[:, hidden_units : 2 * hidden_units]
    back_hidden = total[:, 2 * hidden_units :]
    sigmoid_part = jax.nn.sigmoid(gate_part)
    silu = gate_part * sigmoid_part
    hidden = (silu * up_part).astype(BF16)
    derivative = sigmoid_part * (1.0 + gate_part * (1.0 - sigmoid_part))
    pre_gate = (back_hidden * up_part * derivative).astype(BF16)
    pre_up = (back_hidden * silu).astype(BF16)
    both = jnp.concatenate([pre_gate, pre_up], axis=1).T
    hidden_t = hidden.T

    def one_block(b, carry):
        ins = jnp.dot(both, block(rows_buf, b), preferred_element_type=F32).astype(BF16)
        outs = jnp.dot(hidden_t, block(scaled_buf, b), preferred_element_type=F32).astype(BF16)
        for j in range(halves):
            cols = pl.ds(offset(b, j), half)
            cut = slice(j * half, (j + 1) * half)
            out_ref[0, 0, :, cols] = ins[:hidden_units, cut]
            out_ref[0, 1, :, cols] = ins[hidden_units:, cut]
            out_ref[0, 2, :, cols] = outs[:, cut]
        return carry

    lax.fori_loop(0, blocks, one_block, 0)


def per_device(tokens, cotangent, routes, gates, expert_weights):
    groups = lax.axis_size("expert")
    ring_size = lax.axis_size("ring")
    slots = groups * CAP
    width = tokens.shape[1]
    send = pl.pallas_call(
        pack_kernel, out_shape=jax.ShapeDtypeStruct((2, slots, 2 * width), BF16)
    )(routes.T, gates.T, tokens, cotangent)
    around = [
        (z * 2 + c, ((z + 1 - 2 * c) % ring_size) * 2 + c)
        for z in range(ring_size)
        for c in range(2)
    ]

    def swapped(x):
        return lax.ppermute(x, "core", [(0, 1), (1, 0)])

    own = lax.all_to_all(
        send.reshape(2 * groups, CAP, 2 * width),
        ("half", "expert"),
        split_axis=0,
        concat_axis=0,
        tiled=True,
    ).reshape(1, 2, slots, 2 * width)
    other = swapped(own)
    chains = []
    for m in range(2):
        cut = slice(m * width, (m + 1) * width)
        chains.append([jnp.concatenate([own[..., cut], other[..., cut]], axis=0)])
    turned = [[], []]
    for step in range(1, ring_size // 2 + 1):
        for m in range(2):
            held = chains[m][-1]
            moved = held if step < ring_size // 2 else held[:1]
            moved = lax.ppermute(moved, ("ring", "core"), around)
            if step > 1:
                moved, crossed = lax.optimization_barrier((moved, swapped(held)))
                turned[m].append(crossed)
            chains[m].append(moved)
    for m in range(2):
        last = chains[m].pop()
        chains[m] += turned[m] + [last, swapped(last)]
    sources, parts, first = [], [], 0
    for a, b in zip(*chains):
        sources += [a, b]
        parts.append((first, a.shape[0]))
        first += a.shape[0]
    index = jnp.stack([lax.axis_index("ring"), lax.axis_index("core")]).astype(jnp.int32)
    hidden_units = expert_weights.shape[2]
    any_spec = pl.BlockSpec(memory_space=pl.ANY)
    return pl.pallas_call(
        lambda *refs: grads_kernel(ring_size, parts, *refs),
        out_shape=jax.ShapeDtypeStruct(expert_weights.shape, BF16),
        in_specs=[pl.BlockSpec(memory_space=pltpu.SMEM), any_spec] + [any_spec] * len(sources),
        out_specs=pl.BlockSpec(memory_space=pltpu.VMEM),
        scratch_shapes=[
            pltpu.VMEM((first, 2, slots, width), BF16),
            pltpu.VMEM((first, 2, slots, width), BF16),
            pltpu.VMEM(expert_weights.shape, BF16),
            pltpu.VMEM((slots, 3 * hidden_units), F32),
            pltpu.SemaphoreType.DMA((len(sources),)),
            pltpu.SemaphoreType.DMA,
        ],
        compiler_params=pltpu.CompilerParams(vmem_limit_bytes=60 << 20),
    )(index, expert_weights, *sources)


def solution(mesh):
    sizes = dict(zip(mesh.axis_names, mesh.devices.shape))
    fine = Mesh(
        mesh.devices.reshape(2, sizes["dp"] // 4, 2, sizes["expert"]),
        ("half", "ring", "core", "expert"),
    )
    dp = ("half", "ring", "core")
    return jax.shard_map(
        per_device,
        mesh=fine,
        in_specs=(
            P("expert", dp),
            P("expert", dp),
            P("expert", None),
            P("expert", None),
            P("expert", None, dp, None),
        ),
        out_specs=P("expert", None, dp, None),
        check_vma=False,
    )
```

```python
import jax
import jax.numpy as jnp
from jax import lax
from jax.experimental import pallas as pl
from jax.experimental.pallas import tpu as pltpu
from jax.sharding import Mesh
from jax.sharding import PartitionSpec as P

CAP = 40
BF16 = jnp.bfloat16
F32 = jnp.float32


def pack_kernel(routes_ref, gates_ref, tokens_ref, cotangent_ref, out_ref):
    tokens = routes_ref.shape[1]
    copies, slots, width = out_ref.shape
    experts = slots // CAP
    ids = lax.broadcasted_iota(jnp.int32, (experts, tokens), 0)
    named = jnp.zeros((experts, tokens), F32)
    weight = jnp.zeros((experts, tokens), F32)
    for k in range(routes_ref.shape[0]):
        hit = routes_ref[k : k + 1, :] == ids
        named = named + jnp.where(hit, 1.0, 0.0)
        weight = weight + jnp.where(hit, gates_ref[k : k + 1, :], 0.0)
    down = lax.broadcasted_iota(jnp.int32, (tokens, tokens), 0)
    across = lax.broadcasted_iota(jnp.int32, (tokens, tokens), 1)
    before = jnp.where(down < across, 1.0, 0.0).astype(BF16)
    earlier = jnp.dot(named.astype(BF16), before, preferred_element_type=F32)
    place = jnp.where(named > 0.0, earlier, -1.0)
    places = lax.broadcasted_iota(jnp.int32, (CAP, tokens), 0).astype(F32)
    select, weights = [], []
    for e in range(experts):
        hit = place[e : e + 1, :] == places
        select.append(jnp.where(hit, 1.0, 0.0))
        weights.append(jnp.sum(jnp.where(hit, weight[e : e + 1, :], 0.0), axis=1, keepdims=True))
    select = jnp.concatenate(select, axis=0).astype(BF16)
    weights = jnp.concatenate(weights, axis=0)
    rows = jnp.dot(select, tokens_ref[...], preferred_element_type=F32).astype(BF16)
    scaled = jnp.dot(select, cotangent_ref[...], preferred_element_type=F32)
    scaled = (scaled * weights).astype(BF16)
    for j in range(copies):
        out_ref[j, :, : width // 2] = rows
        out_ref[j, :, width // 2 :] = scaled


def fetch(sources, buffers, sems):
    copies = []
    for n, (source, place) in enumerate(zip(sources, buffers)):
        copy = pltpu.make_async_copy(source, place, sems.at[n])
        copy.start()
        copies.append(copy)
    return copies


def column(index_ref, ring_size, half, b, j):
    ring, core = index_ref[0], index_ref[1]
    far = ring_size // 2
    t, i = b // 2, b % 2
    turned = 1 if t >= far else 0
    step = far if t == ring_size - 1 else t - turned * (far - 1)
    flip = 0 if t == ring_size - 1 else turned
    way = (1 - 2 * core) * (1 - 2 * turned)
    z = lax.rem(ring - way * step + 2 * ring_size, ring_size)
    other = (flip + i) % 2
    c = core + other - 2 * core * other
    return pl.multiple_of(((j * ring_size + z) * 2 + c) * half, half)


def add_forward(index_ref, ring_size, weights_buf, total, rows, scaled, b):
    halves, half = rows.shape[0], rows.shape[2]
    hidden_units = weights_buf.shape[2]
    along = (((1,), (1,)), ((), ()))

    def weight_block(m):
        return jnp.concatenate(
            [
                weights_buf[0, m, :, pl.ds(column(index_ref, ring_size, half, b, j), half)]
                for j in range(halves)
            ],
            axis=1,
        )

    def block(ref):
        return jnp.concatenate([ref[j] for j in range(halves)], axis=1)

    pair = jnp.concatenate([weight_block(0), weight_block(1)], axis=0)
    total[:, : 2 * hidden_units] += lax.dot_general(
        block(rows), pair, along, preferred_element_type=F32
    )
    total[:, 2 * hidden_units :] += lax.dot_general(
        block(scaled), weight_block(2), along, preferred_element_type=F32
    )


def forward_kernel(ring_size, parts, index_ref, weights_ref, *refs):
    count = 2 * len(parts)
    sources, total = refs[:count], refs[count]
    rows_buf, scaled_buf, weights_buf, sems = refs[count + 1 :]
    places, at = [], 0
    for first, size in parts:
        places += [rows_buf.at[pl.ds(at, size)], scaled_buf.at[pl.ds(at, size)]]
        at += size
    copies = fetch((weights_ref,) + sources, [weights_buf] + places, sems)
    total[...] = jnp.zeros_like(total)
    copies[0].wait()
    at = 0
    for n, (first, size) in enumerate(parts):
        copies[1 + 2 * n].wait()
        copies[2 + 2 * n].wait()
        for b in range(size):
            add_forward(
                index_ref, ring_size, weights_buf, total,
                rows_buf.at[at + b], scaled_buf.at[at + b], first + b,
            )
        at += size


def grads_kernel(ring_size, parts, early, index_ref, weights_ref, partial_ref, *refs):
    count = 2 * len(parts)
    sources, out_ref = refs[:count], refs[count]
    rows_buf, scaled_buf, weights_buf, total, sems = refs[count + 1 :]
    halves, half = rows_buf.shape[1], rows_buf.shape[3]
    late = [n for n in range(len(parts)) if n not in early]
    order = late + list(early)
    places, ordered = [], []
    for n in order:
        first, size = parts[n]
        places += [rows_buf.at[pl.ds(first, size)], scaled_buf.at[pl.ds(first, size)]]
        ordered += [sources[2 * n], sources[2 * n + 1]]
    copies = fetch(
        [weights_ref, partial_ref] + ordered, [weights_buf, total] + places, sems
    )
    copies[0].wait()
    copies[1].wait()
    hidden_units = weights_buf.shape[2]
    for k, n in enumerate(late):
        first, size = parts[n]
        copies[2 + 2 * k].wait()
        copies[3 + 2 * k].wait()
        for b in range(first, first + size):
            add_forward(
                index_ref, ring_size, weights_buf, total, rows_buf.at[b], scaled_buf.at[b], b
            )
    gate_part = total[:, :hidden_units]
    up_part = total[:, hidden_units : 2 * hidden_units]
    back_hidden = total[:, 2 * hidden_units :]
    sigmoid_part = jax.nn.sigmoid(gate_part)
    silu = gate_part * sigmoid_part
    hidden = (silu * up_part).astype(BF16)
    derivative = sigmoid_part * (1.0 + gate_part * (1.0 - sigmoid_part))
    pre_gate = (back_hidden * up_part * derivative).astype(BF16)
    pre_up = (back_hidden * silu).astype(BF16)
    both = jnp.concatenate([pre_gate, pre_up], axis=1).T
    hidden_t = hidden.T

    def block(buf, b):
        return jnp.concatenate([buf[b, j] for j in range(halves)], axis=1)

    for k, n in enumerate(order):
        first, size = parts[n]
        if n in early:
            copies[2 + 2 * k].wait()
            copies[3 + 2 * k].wait()
        for b in range(first, first + size):
            ins = jnp.dot(both, block(rows_buf, b), preferred_element_type=F32).astype(BF16)
            outs = jnp.dot(hidden_t, block(scaled_buf, b), preferred_element_type=F32).astype(BF16)
            for j in range(halves):
                cols = pl.ds(column(index_ref, ring_size, half, b, j), half)
                cut = slice(j * half, (j + 1) * half)
                out_ref[0, 0, :, cols] = ins[:hidden_units, cut]
                out_ref[0, 1, :, cols] = ins[hidden_units:, cut]
                out_ref[0, 2, :, cols] = outs[:, cut]


def device_step(tokens, cotangent, routes, gates, expert_weights):
    groups = lax.axis_size("expert")
    ring_size = lax.axis_size("ring")
    slots = groups * CAP
    width = tokens.shape[1]
    send = pl.pallas_call(
        pack_kernel, out_shape=jax.ShapeDtypeStruct((2, slots, 2 * width), BF16)
    )(routes.T, gates.T, tokens, cotangent)
    around = [
        (z * 2 + c, ((z + 1 - 2 * c) % ring_size) * 2 + c)
        for z in range(ring_size)
        for c in range(2)
    ]

    def swapped(x):
        return lax.ppermute(x, "core", [(0, 1), (1, 0)])

    own = lax.all_to_all(
        send.reshape(2 * groups, CAP, 2 * width),
        ("half", "expert"),
        split_axis=0,
        concat_axis=0,
        tiled=True,
    ).reshape(1, 2, slots, 2 * width)
    other = swapped(own)
    chains = []
    for m in range(2):
        cut = slice(m * width, (m + 1) * width)
        chains.append([jnp.concatenate([own[..., cut], other[..., cut]], axis=0)])
    turned, raw = [[], []], [[], []]
    far = ring_size // 2
    for step in range(1, far + 1):
        for m in range(2):
            held = chains[m][-1]
            moved = held if step < far else held[:1]
            moved = lax.ppermute(moved, ("ring", "core"), around)
            if step > 1:
                crossed = swapped(held)
                raw[m].append(crossed)
                moved, crossed = lax.optimization_barrier((moved, crossed))
                turned[m].append(crossed)
            chains[m].append(moved)
    near = [chain[: far - 1] for chain in chains]
    for m in range(2):
        last = chains[m].pop()
        chains[m] += turned[m] + [last, swapped(last)]
    parts, first = [], 0
    for piece in chains[0]:
        parts.append((first, piece.shape[0]))
        first += piece.shape[0]
    early = list(range(far - 1)) + list(range(far, 2 * far - 2))
    index = jnp.stack([lax.axis_index("ring"), lax.axis_index("core")]).astype(jnp.int32)
    hidden_units = expert_weights.shape[2]
    features = expert_weights.shape[3]
    any_spec = pl.BlockSpec(memory_space=pl.ANY)
    smem_spec = pl.BlockSpec(memory_space=pltpu.SMEM)
    early_parts = [parts[n] for n in early]
    early_blocks = sum(size for _, size in early_parts)
    sources = []
    for a, b in zip(near[0] + raw[0][: far - 2], near[1] + raw[1][: far - 2]):
        sources += [a, b]
    piece_bytes = 4 * slots * width
    weight_bytes = 6 * hidden_units * features
    block_flops = 12 * slots * width * hidden_units
    partial = pl.pallas_call(
        lambda *refs: forward_kernel(ring_size, early_parts, *refs),
        out_shape=jax.ShapeDtypeStruct((slots, 3 * hidden_units), F32),
        in_specs=[smem_spec, any_spec] + [any_spec] * len(sources),
        out_specs=pl.BlockSpec(memory_space=pltpu.VMEM),
        scratch_shapes=[
            pltpu.VMEM((early_blocks, 2, slots, width), BF16),
            pltpu.VMEM((early_blocks, 2, slots, width), BF16),
            pltpu.VMEM(expert_weights.shape, BF16),
            pltpu.SemaphoreType.DMA((1 + len(sources),)),
        ],
        cost_estimate=pl.CostEstimate(
            flops=early_blocks * block_flops,
            bytes_accessed=2 * early_blocks * piece_bytes + weight_bytes,
            transcendentals=0,
        ),
        compiler_params=pltpu.CompilerParams(vmem_limit_bytes=60 << 20),
    )(index, expert_weights, *sources)
    sources = []
    for a, b in zip(*chains):
        sources += [a, b]
    return pl.pallas_call(
        lambda *refs: grads_kernel(ring_size, parts, early, *refs),
        out_shape=jax.ShapeDtypeStruct(expert_weights.shape, BF16),
        in_specs=[smem_spec, any_spec, any_spec] + [any_spec] * len(sources),
        out_specs=pl.BlockSpec(memory_space=pltpu.VMEM),
        scratch_shapes=[
            pltpu.VMEM((first, 2, slots, width), BF16),
            pltpu.VMEM((first, 2, slots, width), BF16),
            pltpu.VMEM(expert_weights.shape, BF16),
            pltpu.VMEM((slots, 3 * hidden_units), F32),
            pltpu.SemaphoreType.DMA((2 + len(sources),)),
        ],
        cost_estimate=pl.CostEstimate(
            flops=(2 * first - early_blocks) * block_flops,
            bytes_accessed=2 * first * piece_bytes + 2 * weight_bytes,
            transcendentals=slots * hidden_units,
        ),
        compiler_params=pltpu.CompilerParams(vmem_limit_bytes=60 << 20),
    )(index, expert_weights, partial, *sources)


def solution(mesh):
    sizes = dict(zip(mesh.axis_names, mesh.devices.shape))
    fine = Mesh(
        mesh.devices.reshape(2, sizes["dp"] // 4, 2, sizes["expert"]),
        ("half", "ring", "core", "expert"),
    )
    dp = ("half", "ring", "core")
    return jax.shard_map(
        device_step,
        mesh=fine,
        in_specs=(
            P("expert", dp),
            P("expert", dp),
            P("expert", None),
            P("expert", None),
            P("expert", None, dp, None),
        ),
        out_specs=P("expert", None, dp, None),
        check_vma=False,
    )
```

```python
import functools

import jax
import jax.numpy as jnp
from jax import lax
from jax.experimental import pallas as pl
from jax.experimental.pallas import tpu as pltpu
from jax.sharding import Mesh
from jax.sharding import PartitionSpec as P

CAP = 40
BF16 = jnp.bfloat16
F32 = jnp.float32
EARLY_VMEM = 12 << 20
GRADS_VMEM = 18 << 20


def pack_kernel(routes_ref, gates_ref, tokens_ref, cotangent_ref, out_ref):
    tokens = routes_ref.shape[1]
    copies, slots, width = out_ref.shape
    experts = slots // CAP
    ids = lax.broadcasted_iota(jnp.int32, (experts, tokens), 0)
    named = jnp.zeros((experts, tokens), F32)
    weight = jnp.zeros((experts, tokens), F32)
    for k in range(routes_ref.shape[0]):
        hit = routes_ref[k : k + 1, :] == ids
        named = named + jnp.where(hit, 1.0, 0.0)
        weight = weight + jnp.where(hit, gates_ref[k : k + 1, :], 0.0)
    down = lax.broadcasted_iota(jnp.int32, (tokens, tokens), 0)
    across = lax.broadcasted_iota(jnp.int32, (tokens, tokens), 1)
    before = jnp.where(down < across, 1.0, 0.0).astype(BF16)
    earlier = jnp.dot(named.astype(BF16), before, preferred_element_type=F32)
    place = jnp.where(named > 0.0, earlier, -1.0)
    places = lax.broadcasted_iota(jnp.int32, (CAP, tokens), 0).astype(F32)
    select, weights = [], []
    for e in range(experts):
        hit = place[e : e + 1, :] == places
        select.append(jnp.where(hit, 1.0, 0.0))
        weights.append(jnp.sum(jnp.where(hit, weight[e : e + 1, :], 0.0), axis=1, keepdims=True))
    select = jnp.concatenate(select, axis=0).astype(BF16)
    weights = jnp.concatenate(weights, axis=0)
    rows = jnp.dot(select, tokens_ref[...], preferred_element_type=F32).astype(BF16)
    scaled = jnp.dot(select, cotangent_ref[...], preferred_element_type=F32)
    scaled = (scaled * weights).astype(BF16)
    for j in range(copies):
        out_ref[j, :, : width // 2] = rows
        out_ref[j, :, width // 2 :] = scaled


def fetch(sources, buffers, sems):
    copies = []
    for n, (source, place) in enumerate(zip(sources, buffers)):
        copy = pltpu.make_async_copy(source, place, sems.at[n])
        copy.start()
        copies.append(copy)
    return copies


def column(index_ref, ring_size, half, block, j):
    step, chain, turned = block
    ring, core = index_ref[0], index_ref[1]
    way = (1 - 2 * core) * (1 - 2 * turned)
    z = lax.rem(ring - way * step + 2 * ring_size, ring_size)
    other = chain ^ turned
    c = core + other - 2 * core * other
    return pl.multiple_of(((j * ring_size + z) * 2 + c) * half, half)


def add_forward(index_ref, ring_size, weights_buf, total, piece, block):
    halves, half = piece.shape[0], piece.shape[2] // 2
    hidden_units = weights_buf.shape[2]
    along = (((1,), (1,)), ((), ()))

    def weight_block(m):
        return jnp.concatenate(
            [
                weights_buf[0, m, :, pl.ds(column(index_ref, ring_size, half, block, j), half)]
                for j in range(halves)
            ],
            axis=1,
        )

    pair = jnp.concatenate([weight_block(0), weight_block(1)], axis=0)
    total[:, : 2 * hidden_units] += lax.dot_general(
        joined(piece, 0), pair, along, preferred_element_type=F32
    )
    total[:, 2 * hidden_units :] += lax.dot_general(
        joined(piece, 1), weight_block(2), along, preferred_element_type=F32
    )


def joined(piece, part):
    halves, half = piece.shape[0], piece.shape[2] // 2
    cut = slice(part * half, (part + 1) * half)
    return jnp.concatenate([piece[j, :, cut] for j in range(halves)], axis=1)


def forward_kernel(ring_size, blocks, index_ref, weights_ref, *refs):
    count = len(blocks)
    sources, total = refs[:count], refs[count]
    pieces_buf, weights_buf, sems = refs[count + 1 :]
    copies = fetch(
        (weights_ref,) + sources, [weights_buf] + [pieces_buf.at[k] for k in range(count)], sems
    )
    total[...] = jnp.zeros_like(total)
    copies[0].wait()
    for k, block in enumerate(blocks):
        copies[1 + k].wait()
        add_forward(index_ref, ring_size, weights_buf, total, pieces_buf.at[k], block)


def grads_kernel(ring_size, blocks, early, sums, index_ref, weights_ref, *refs):
    count = len(blocks)
    partials, sources, out_ref = refs[:sums], refs[sums : sums + count], refs[sums + count]
    pieces_buf, weights_buf, partial_buf, total, sems = refs[sums + count + 1 :]
    half = pieces_buf.shape[3] // 2
    halves = pieces_buf.shape[1]
    late = [k for k in range(count) if blocks[k] not in early]
    order = late + [k for k in range(count) if blocks[k] in early]
    base = 1 + sums
    copies = fetch(
        [weights_ref] + list(partials) + [sources[k] for k in order],
        [weights_buf] + [partial_buf.at[m] for m in range(sums)] + [pieces_buf.at[k] for k in order],
        sems,
    )
    for copy in copies[:base]:
        copy.wait()
    running = partial_buf[0]
    for m in range(1, sums):
        running = running + partial_buf[m]
    total[...] = running
    hidden_units = weights_buf.shape[2]
    for n, k in enumerate(late):
        copies[base + n].wait()
        add_forward(index_ref, ring_size, weights_buf, total, pieces_buf.at[k], blocks[k])
    gate_part = total[:, :hidden_units]
    up_part = total[:, hidden_units : 2 * hidden_units]
    back_hidden = total[:, 2 * hidden_units :]
    sigmoid_part = jax.nn.sigmoid(gate_part)
    silu = gate_part * sigmoid_part
    hidden = (silu * up_part).astype(BF16)
    derivative = sigmoid_part * (1.0 + gate_part * (1.0 - sigmoid_part))
    pre_gate = (back_hidden * up_part * derivative).astype(BF16)
    pre_up = (back_hidden * silu).astype(BF16)
    both = jnp.concatenate([pre_gate, pre_up], axis=1).T
    hidden_t = hidden.T
    for n, k in enumerate(order):
        if n >= len(late):
            copies[base + n].wait()
        piece = pieces_buf.at[k]
        ins = jnp.dot(both, joined(piece, 0), preferred_element_type=F32).astype(BF16)
        outs = jnp.dot(hidden_t, joined(piece, 1), preferred_element_type=F32).astype(BF16)
        for j in range(halves):
            cols = pl.ds(column(index_ref, ring_size, half, blocks[k], j), half)
            cut = slice(j * half, (j + 1) * half)
            out_ref[0, 0, :, cols] = ins[:hidden_units, cut]
            out_ref[0, 1, :, cols] = ins[hidden_units:, cut]
            out_ref[0, 2, :, cols] = outs[:, cut]


def device_step(tokens, cotangent, routes, gates, expert_weights):
    groups = lax.axis_size("expert")
    ring_size = lax.axis_size("ring")
    slots = groups * CAP
    width = tokens.shape[1]
    send = pl.pallas_call(
        pack_kernel, out_shape=jax.ShapeDtypeStruct((2, slots, 2 * width), BF16)
    )(routes.T, gates.T, tokens, cotangent)
    around = [
        (z * 2 + c, ((z + 1 - 2 * c) % ring_size) * 2 + c)
        for z in range(ring_size)
        for c in range(2)
    ]

    def swapped(x):
        return lax.ppermute(x, "core", [(0, 1), (1, 0)])

    own = lax.all_to_all(
        send.reshape(2 * groups, CAP, 2 * width),
        ("half", "expert"),
        split_axis=0,
        concat_axis=0,
        tiled=True,
    ).reshape(2, slots, 2 * width)
    far = ring_size // 2
    held = {(0, 0, 0): own, (0, 1, 0): swapped(own)}
    raw = {}
    for step in range(1, far + 1):
        for chain in range(2 if step < far else 1):
            piece = lax.ppermute(held[step - 1, chain, 0], ("ring", "core"), around)
            raw[step, chain, 0] = piece
            if step > 1:
                crossed = swapped(held[step - 1, chain, 0])
                raw[step - 1, chain, 1] = crossed
                piece, crossed = lax.optimization_barrier((piece, crossed))
                held[step - 1, chain, 1] = crossed
            held[step, chain, 0] = piece
    held[far - 1, 1, 1] = swapped(held[far - 1, 1, 0])
    held[far, 0, 1] = swapped(held[far, 0, 0])
    blocks = list(held)
    index = jnp.stack([lax.axis_index("ring"), lax.axis_index("core")]).astype(jnp.int32)
    hidden_units = expert_weights.shape[2]
    features = expert_weights.shape[3]
    any_spec = pl.BlockSpec(memory_space=pl.ANY)
    smem_spec = pl.BlockSpec(memory_space=pltpu.SMEM)
    piece_bytes = 8 * slots * width
    weight_bytes = 6 * hidden_units * features
    block_flops = 12 * slots * width * hidden_units
    groups_early = [
        [(0, 0, 0), (0, 1, 0)],
        [(s, c, t) for s in range(1, far - 1) for t in range(2) for c in range(2)],
    ]
    groups_early = [g for g in groups_early if g]
    partials = []
    for chosen in groups_early:
        partials.append(
            pl.pallas_call(
                functools.partial(forward_kernel, ring_size, chosen),
                out_shape=jax.ShapeDtypeStruct((slots, 3 * hidden_units), F32),
                in_specs=[smem_spec, any_spec] + [any_spec] * len(chosen),
                out_specs=pl.BlockSpec(memory_space=pltpu.VMEM),
                scratch_shapes=[
                    pltpu.VMEM((len(chosen), 2, slots, 2 * width), BF16),
                    pltpu.VMEM(expert_weights.shape, BF16),
                    pltpu.SemaphoreType.DMA((1 + len(chosen),)),
                ],
                cost_estimate=pl.CostEstimate(
                    flops=len(chosen) * block_flops,
                    bytes_accessed=len(chosen) * piece_bytes + weight_bytes,
                    transcendentals=0,
                ),
                compiler_params=pltpu.CompilerParams(vmem_limit_bytes=EARLY_VMEM),
            )(index, expert_weights, *[raw.get(k, held[k]) for k in chosen])
        )
    early = [k for g in groups_early for k in g]
    return pl.pallas_call(
        functools.partial(grads_kernel, ring_size, blocks, early, len(partials)),
        out_shape=jax.ShapeDtypeStruct(expert_weights.shape, BF16),
        in_specs=[smem_spec, any_spec] + [any_spec] * (len(partials) + len(blocks)),
        out_specs=pl.BlockSpec(memory_space=pltpu.VMEM),
        scratch_shapes=[
            pltpu.VMEM((len(blocks), 2, slots, 2 * width), BF16),
            pltpu.VMEM(expert_weights.shape, BF16),
            pltpu.VMEM((len(partials), slots, 3 * hidden_units), F32),
            pltpu.VMEM((slots, 3 * hidden_units), F32),
            pltpu.SemaphoreType.DMA((1 + len(partials) + len(blocks),)),
        ],
        cost_estimate=pl.CostEstimate(
            flops=2 * len(blocks) * block_flops,
            bytes_accessed=len(blocks) * piece_bytes + 2 * weight_bytes,
            transcendentals=slots * hidden_units,
        ),
        compiler_params=pltpu.CompilerParams(vmem_limit_bytes=GRADS_VMEM),
    )(index, expert_weights, *partials, *[held[k] for k in blocks])


def solution(mesh):
    sizes = dict(zip(mesh.axis_names, mesh.devices.shape))
    fine = Mesh(
        mesh.devices.reshape(2, sizes["dp"] // 4, 2, sizes["expert"]),
        ("half", "ring", "core", "expert"),
    )
    dp = ("half", "ring", "core")
    return jax.shard_map(
        device_step,
        mesh=fine,
        in_specs=(
            P("expert", dp),
            P("expert", dp),
            P("expert", None),
            P("expert", None),
            P("expert", None, dp, None),
        ),
        out_specs=P("expert", None, dp, None),
        check_vma=False,
    )
```

```python
import functools

import jax
import jax.numpy as jnp
from jax import lax
from jax.experimental import pallas as pl
from jax.experimental.pallas import tpu as pltpu
from jax.sharding import Mesh
from jax.sharding import PartitionSpec as P

CAP = 40
BF16 = jnp.bfloat16
F32 = jnp.float32
EARLY_VMEM = 60 << 20
GRADS_VMEM = 60 << 20
FORWARD_GROUP = 4
GRADS_GROUP = 4


def pack_kernel(routes_ref, gates_ref, tokens_ref, cotangent_ref, out_ref):
    tokens = routes_ref.shape[1]
    copies, slots, width = out_ref.shape
    experts = slots // CAP
    ids = lax.broadcasted_iota(jnp.int32, (experts, tokens), 0)
    named = jnp.zeros((experts, tokens), F32)
    weight = jnp.zeros((experts, tokens), F32)
    for k in range(routes_ref.shape[0]):
        hit = routes_ref[k : k + 1, :] == ids
        named = named + jnp.where(hit, 1.0, 0.0)
        weight = weight + jnp.where(hit, gates_ref[k : k + 1, :], 0.0)
    down = lax.broadcasted_iota(jnp.int32, (tokens, tokens), 0)
    across = lax.broadcasted_iota(jnp.int32, (tokens, tokens), 1)
    before = jnp.where(down < across, 1.0, 0.0).astype(BF16)
    earlier = jnp.dot(named.astype(BF16), before, preferred_element_type=F32)
    place = jnp.where(named > 0.0, earlier, -1.0)
    places = lax.broadcasted_iota(jnp.int32, (CAP, tokens), 0).astype(F32)
    select, weights = [], []
    for e in range(experts):
        hit = place[e : e + 1, :] == places
        select.append(jnp.where(hit, 1.0, 0.0))
        weights.append(jnp.sum(jnp.where(hit, weight[e : e + 1, :], 0.0), axis=1, keepdims=True))
    select = jnp.concatenate(select, axis=0).astype(BF16)
    weights = jnp.concatenate(weights, axis=0)
    rows = jnp.dot(select, tokens_ref[...], preferred_element_type=F32).astype(BF16)
    scaled = jnp.dot(select, cotangent_ref[...], preferred_element_type=F32)
    scaled = (scaled * weights).astype(BF16)
    for j in range(copies):
        out_ref[j, :, : width // 2] = rows
        out_ref[j, :, width // 2 :] = scaled


def fetch(sources, buffers, sems):
    copies = []
    for n, (source, place) in enumerate(zip(sources, buffers)):
        copy = pltpu.make_async_copy(source, place, sems.at[n])
        copy.start()
        copies.append(copy)
    return copies


def column(index_ref, ring_size, half, block, j):
    step, chain, turned = block
    ring, core = index_ref[0], index_ref[1]
    way = (1 - 2 * core) * (1 - 2 * turned)
    z = lax.rem(ring - way * step + 2 * ring_size, ring_size)
    other = chain ^ turned
    c = core + other - 2 * core * other
    return pl.multiple_of(((j * ring_size + z) * 2 + c) * half, half)


def joined(pieces, part):
    half = pieces[0].shape[2] // 2
    cut = slice(part * half, (part + 1) * half)
    return jnp.concatenate(
        [piece[j, :, cut] for piece in pieces for j in range(piece.shape[0])], axis=1
    )


def add_forward(index_ref, ring_size, weights_buf, total, pieces, blocks):
    halves, half = pieces[0].shape[0], pieces[0].shape[2] // 2
    hidden_units = weights_buf.shape[2]
    along = (((1,), (1,)), ((), ()))

    def weight_block(m):
        return jnp.concatenate(
            [
                weights_buf[0, m, :, pl.ds(column(index_ref, ring_size, half, block, j), half)]
                for block in blocks
                for j in range(halves)
            ],
            axis=1,
        )

    pair = jnp.concatenate([weight_block(0), weight_block(1)], axis=0)
    total[:, : 2 * hidden_units] += lax.dot_general(
        joined(pieces, 0), pair, along, preferred_element_type=F32
    )
    total[:, 2 * hidden_units :] += lax.dot_general(
        joined(pieces, 1), weight_block(2), along, preferred_element_type=F32
    )


def forward_kernel(ring_size, blocks, index_ref, weights_ref, *refs):
    count = len(blocks)
    sources, total = refs[:count], refs[count]
    pieces_buf, weights_buf, sems = refs[count + 1 :]
    copies = fetch(
        (weights_ref,) + sources, [weights_buf] + [pieces_buf.at[k] for k in range(count)], sems
    )
    total[...] = jnp.zeros_like(total)
    copies[0].wait()
    for k in range(0, count, FORWARD_GROUP):
        chosen = range(k, min(k + FORWARD_GROUP, count))
        for n in chosen:
            copies[1 + n].wait()
        add_forward(
            index_ref, ring_size, weights_buf, total,
            [pieces_buf.at[n] for n in chosen], [blocks[n] for n in chosen],
        )


def grads_kernel(ring_size, blocks, early, sums, index_ref, weights_ref, *refs):
    count = len(blocks)
    partials, sources, out_ref = refs[:sums], refs[sums : sums + count], refs[sums + count]
    pieces_buf, weights_buf, partial_buf, total, sems = refs[sums + count + 1 :]
    half = pieces_buf.shape[3] // 2
    halves = pieces_buf.shape[1]
    late = [k for k in range(count) if blocks[k] not in early]
    order = late + [k for k in range(count) if blocks[k] in early]
    base = 1 + sums
    copies = fetch(
        [weights_ref] + list(partials) + [sources[k] for k in order],
        [weights_buf] + [partial_buf.at[m] for m in range(sums)] + [pieces_buf.at[k] for k in order],
        sems,
    )
    for copy in copies[:base]:
        copy.wait()
    running = partial_buf[0]
    for m in range(1, sums):
        running = running + partial_buf[m]
    total[...] = running
    hidden_units = weights_buf.shape[2]
    for n in range(0, len(late), FORWARD_GROUP):
        chosen = late[n : n + FORWARD_GROUP]
        for m in range(len(chosen)):
            copies[base + n + m].wait()
        add_forward(
            index_ref, ring_size, weights_buf, total,
            [pieces_buf.at[k] for k in chosen], [blocks[k] for k in chosen],
        )
    gate_part = total[:, :hidden_units]
    up_part = total[:, hidden_units : 2 * hidden_units]
    back_hidden = total[:, 2 * hidden_units :]
    sigmoid_part = jax.nn.sigmoid(gate_part)
    silu = gate_part * sigmoid_part
    hidden = (silu * up_part).astype(BF16)
    derivative = sigmoid_part * (1.0 + gate_part * (1.0 - sigmoid_part))
    pre_gate = (back_hidden * up_part * derivative).astype(BF16)
    pre_up = (back_hidden * silu).astype(BF16)
    both = jnp.concatenate([pre_gate, pre_up], axis=1).T
    hidden_t = hidden.T
    for n in range(0, count, GRADS_GROUP):
        chosen = order[n : n + GRADS_GROUP]
        for m in range(len(chosen)):
            if n + m >= len(late):
                copies[base + n + m].wait()
        pieces = [pieces_buf.at[k] for k in chosen]
        ins = jnp.dot(both, joined(pieces, 0), preferred_element_type=F32).astype(BF16)
        outs = jnp.dot(hidden_t, joined(pieces, 1), preferred_element_type=F32).astype(BF16)
        for m, k in enumerate(chosen):
            for j in range(halves):
                cols = pl.ds(column(index_ref, ring_size, half, blocks[k], j), half)
                cut = slice((m * halves + j) * half, (m * halves + j + 1) * half)
                out_ref[0, 0, :, cols] = ins[:hidden_units, cut]
                out_ref[0, 1, :, cols] = ins[hidden_units:, cut]
                out_ref[0, 2, :, cols] = outs[:, cut]


def device_step(tokens, cotangent, routes, gates, expert_weights):
    groups = lax.axis_size("expert")
    ring_size = lax.axis_size("ring")
    slots = groups * CAP
    width = tokens.shape[1]
    send = pl.pallas_call(
        pack_kernel, out_shape=jax.ShapeDtypeStruct((2, slots, 2 * width), BF16)
    )(routes.T, gates.T, tokens, cotangent)
    around = [
        (z * 2 + c, ((z + 1 - 2 * c) % ring_size) * 2 + c)
        for z in range(ring_size)
        for c in range(2)
    ]

    def swapped(x):
        return lax.ppermute(x, "core", [(0, 1), (1, 0)])

    own = lax.all_to_all(
        send.reshape(2 * groups, CAP, 2 * width),
        ("half", "expert"),
        split_axis=0,
        concat_axis=0,
        tiled=True,
    ).reshape(2, slots, 2 * width)
    far = ring_size // 2
    held = {(0, 0, 0): own, (0, 1, 0): swapped(own)}
    raw = {}
    for step in range(1, far + 1):
        for chain in range(2 if step < far else 1):
            piece = lax.ppermute(held[step - 1, chain, 0], ("ring", "core"), around)
            raw[step, chain, 0] = piece
            if step > 1:
                crossed = swapped(held[step - 1, chain, 0])
                raw[step - 1, chain, 1] = crossed
                piece, crossed = lax.optimization_barrier((piece, crossed))
                held[step - 1, chain, 1] = crossed
            held[step, chain, 0] = piece
    held[far - 1, 1, 1] = swapped(held[far - 1, 1, 0])
    held[far, 0, 1] = swapped(held[far, 0, 0])
    blocks = list(held)
    index = jnp.stack([lax.axis_index("ring"), lax.axis_index("core")]).astype(jnp.int32)
    hidden_units = expert_weights.shape[2]
    features = expert_weights.shape[3]
    any_spec = pl.BlockSpec(memory_space=pl.ANY)
    smem_spec = pl.BlockSpec(memory_space=pltpu.SMEM)
    piece_bytes = 8 * slots * width
    weight_bytes = 6 * hidden_units * features
    block_flops = 12 * slots * width * hidden_units
    groups_early = [
        [(0, 0, 0), (0, 1, 0)],
        [(s, c, t) for s in range(1, far - 1) for t in range(2) for c in range(2)],
    ]
    groups_early = [g for g in groups_early if g]
    partials = []
    for chosen in groups_early:
        partials.append(
            pl.pallas_call(
                functools.partial(forward_kernel, ring_size, chosen),
                out_shape=jax.ShapeDtypeStruct((slots, 3 * hidden_units), F32),
                in_specs=[smem_spec, any_spec] + [any_spec] * len(chosen),
                out_specs=pl.BlockSpec(memory_space=pltpu.VMEM),
                scratch_shapes=[
                    pltpu.VMEM((len(chosen), 2, slots, 2 * width), BF16),
                    pltpu.VMEM(expert_weights.shape, BF16),
                    pltpu.SemaphoreType.DMA((1 + len(chosen),)),
                ],
                cost_estimate=pl.CostEstimate(
                    flops=len(chosen) * block_flops,
                    bytes_accessed=len(chosen) * piece_bytes + weight_bytes,
                    transcendentals=0,
                ),
                compiler_params=pltpu.CompilerParams(vmem_limit_bytes=EARLY_VMEM),
            )(index, expert_weights, *[raw.get(k, held[k]) for k in chosen])
        )
    early = [k for g in groups_early for k in g]
    return pl.pallas_call(
        functools.partial(grads_kernel, ring_size, blocks, early, len(partials)),
        out_shape=jax.ShapeDtypeStruct(expert_weights.shape, BF16),
        in_specs=[smem_spec, any_spec] + [any_spec] * (len(partials) + len(blocks)),
        out_specs=pl.BlockSpec(memory_space=pltpu.VMEM),
        scratch_shapes=[
            pltpu.VMEM((len(blocks), 2, slots, 2 * width), BF16),
            pltpu.VMEM(expert_weights.shape, BF16),
            pltpu.VMEM((len(partials), slots, 3 * hidden_units), F32),
            pltpu.VMEM((slots, 3 * hidden_units), F32),
            pltpu.SemaphoreType.DMA((1 + len(partials) + len(blocks),)),
        ],
        cost_estimate=pl.CostEstimate(
            flops=2 * len(blocks) * block_flops,
            bytes_accessed=len(blocks) * piece_bytes + 2 * weight_bytes,
            transcendentals=slots * hidden_units,
        ),
        compiler_params=pltpu.CompilerParams(vmem_limit_bytes=GRADS_VMEM),
    )(index, expert_weights, *partials, *[held[k] for k in blocks])


def solution(mesh):
    sizes = dict(zip(mesh.axis_names, mesh.devices.shape))
    fine = Mesh(
        mesh.devices.reshape(2, sizes["dp"] // 4, 2, sizes["expert"]),
        ("half", "ring", "core", "expert"),
    )
    dp = ("half", "ring", "core")
    return jax.shard_map(
        device_step,
        mesh=fine,
        in_specs=(
            P("expert", dp),
            P("expert", dp),
            P("expert", None),
            P("expert", None),
            P("expert", None, dp, None),
        ),
        out_specs=P("expert", None, dp, None),
        check_vma=False,
    )
```

```python
import functools

import jax
import jax.numpy as jnp
from jax import lax
from jax.experimental import pallas as pl
from jax.experimental.pallas import tpu as pltpu
from jax.sharding import Mesh
from jax.sharding import PartitionSpec as P

CAP = 40
BF16 = jnp.bfloat16
F32 = jnp.float32
EARLY_VMEM = 8 << 20
GRADS_VMEM = 16 << 20
FORWARD_GROUP = 4
GRADS_GROUP = 4


def pack_kernel(routes_ref, gates_ref, tokens_ref, cotangent_ref, out_ref):
    tokens = routes_ref.shape[1]
    copies, slots, width = out_ref.shape
    experts = slots // CAP
    ids = lax.broadcasted_iota(jnp.int32, (experts, tokens), 0)
    named = jnp.zeros((experts, tokens), F32)
    weight = jnp.zeros((experts, tokens), F32)
    for k in range(routes_ref.shape[0]):
        hit = routes_ref[k : k + 1, :] == ids
        named = named + jnp.where(hit, 1.0, 0.0)
        weight = weight + jnp.where(hit, gates_ref[k : k + 1, :], 0.0)
    down = lax.broadcasted_iota(jnp.int32, (tokens, tokens), 0)
    across = lax.broadcasted_iota(jnp.int32, (tokens, tokens), 1)
    before = jnp.where(down < across, 1.0, 0.0).astype(BF16)
    earlier = jnp.dot(named.astype(BF16), before, preferred_element_type=F32)
    place = jnp.where(named > 0.0, earlier, -1.0)
    places = lax.broadcasted_iota(jnp.int32, (CAP, tokens), 0).astype(F32)
    select, weights = [], []
    for e in range(experts):
        hit = place[e : e + 1, :] == places
        select.append(jnp.where(hit, 1.0, 0.0))
        weights.append(jnp.sum(jnp.where(hit, weight[e : e + 1, :], 0.0), axis=1, keepdims=True))
    select = jnp.concatenate(select, axis=0).astype(BF16)
    weights = jnp.concatenate(weights, axis=0)
    rows = jnp.dot(select, tokens_ref[...], preferred_element_type=F32).astype(BF16)
    scaled = jnp.dot(select, cotangent_ref[...], preferred_element_type=F32)
    scaled = (scaled * weights).astype(BF16)
    for j in range(copies):
        out_ref[j, :, : width // 2] = rows
        out_ref[j, :, width // 2 :] = scaled


def fetch(sources, buffers, sems):
    copies = []
    for n, (source, place) in enumerate(zip(sources, buffers)):
        copy = pltpu.make_async_copy(source, place, sems.at[n])
        copy.start()
        copies.append(copy)
    return copies


def column(index_ref, ring_size, half, block, j):
    step, chain, turned = block
    ring, core = index_ref[0], index_ref[1]
    way = (1 - 2 * core) * (1 - 2 * turned)
    z = lax.rem(ring - way * step + 2 * ring_size, ring_size)
    other = chain ^ turned
    c = core + other - 2 * core * other
    return pl.multiple_of(((j * ring_size + z) * 2 + c) * half, half)


def joined(pieces, part):
    half = pieces[0].shape[2] // 2
    cut = slice(part * half, (part + 1) * half)
    return jnp.concatenate(
        [piece[j, :, cut] for piece in pieces for j in range(piece.shape[0])], axis=1
    )


def weight_copies(index_ref, ring_size, weights_ref, weights_buf, blocks):
    halves, half = weights_buf.shape[1], weights_buf.shape[4]
    sources, places = [], []
    for k, block in enumerate(blocks):
        for j in range(halves):
            cols = pl.ds(column(index_ref, ring_size, half, block, j), half)
            sources.append(weights_ref.at[0, :, :, cols])
            places.append(weights_buf.at[k, j])
    return sources, places


def add_forward(weights_buf, total, pieces, numbers):
    halves, hidden_units = weights_buf.shape[1], weights_buf.shape[3]
    along = (((1,), (1,)), ((), ()))

    def weight_block(m):
        return jnp.concatenate(
            [weights_buf[k, j, m] for k in numbers for j in range(halves)], axis=1
        )

    pair = jnp.concatenate([weight_block(0), weight_block(1)], axis=0)
    total[:, : 2 * hidden_units] += lax.dot_general(
        joined(pieces, 0), pair, along, preferred_element_type=F32
    )
    total[:, 2 * hidden_units :] += lax.dot_general(
        joined(pieces, 1), weight_block(2), along, preferred_element_type=F32
    )


def forward_kernel(ring_size, blocks, chained, index_ref, weights_ref, *refs):
    count = len(blocks)
    partials, sources, total = refs[:chained], refs[chained : chained + count], refs[chained + count]
    pieces_buf, weights_buf, sems = refs[chained + count + 1 :]
    slices, homes = weight_copies(index_ref, ring_size, weights_ref, weights_buf, blocks)
    copies = fetch(
        list(partials) + slices + list(sources),
        [total] * chained + homes + [pieces_buf.at[k] for k in range(count)],
        sems,
    )
    if not chained:
        total[...] = jnp.zeros_like(total)
    base = chained + len(slices)
    for copy in copies[:base]:
        copy.wait()
    for k in range(0, count, FORWARD_GROUP):
        chosen = range(k, min(k + FORWARD_GROUP, count))
        for n in chosen:
            copies[base + n].wait()
        add_forward(weights_buf, total, [pieces_buf.at[n] for n in chosen], chosen)


def grads_kernel(ring_size, blocks, late, index_ref, weights_ref, partial_ref, *refs):
    count = len(blocks)
    sources, out_ref = refs[:count], refs[count]
    pieces_buf, weights_buf, total, sems = refs[count + 1 :]
    half = pieces_buf.shape[3] // 2
    halves = pieces_buf.shape[1]
    hidden_units = weights_buf.shape[3]
    last = [blocks.index(block) for block in late]
    order = last + [k for k in range(count) if k not in last]
    slices, homes = weight_copies(index_ref, ring_size, weights_ref, weights_buf, late)
    copies = fetch(
        [partial_ref] + slices + [sources[k] for k in order],
        [total] + homes + [pieces_buf.at[k] for k in order],
        sems,
    )
    base = 1 + len(slices)
    for copy in copies[: base + len(last)]:
        copy.wait()
    add_forward(weights_buf, total, [pieces_buf.at[k] for k in last], range(len(last)))
    gate_part = total[:, :hidden_units]
    up_part = total[:, hidden_units : 2 * hidden_units]
    back_hidden = total[:, 2 * hidden_units :]
    sigmoid_part = jax.nn.sigmoid(gate_part)
    silu = gate_part * sigmoid_part
    hidden = (silu * up_part).astype(BF16)
    derivative = sigmoid_part * (1.0 + gate_part * (1.0 - sigmoid_part))
    pre_gate = (back_hidden * up_part * derivative).astype(BF16)
    pre_up = (back_hidden * silu).astype(BF16)
    both = jnp.concatenate([pre_gate, pre_up], axis=1).T
    hidden_t = hidden.T
    for n in range(0, count, GRADS_GROUP):
        chosen = order[n : n + GRADS_GROUP]
        for m in range(len(chosen)):
            if n + m >= len(last):
                copies[base + n + m].wait()
        pieces = [pieces_buf.at[k] for k in chosen]
        ins = jnp.dot(both, joined(pieces, 0), preferred_element_type=F32).astype(BF16)
        outs = jnp.dot(hidden_t, joined(pieces, 1), preferred_element_type=F32).astype(BF16)
        for m, k in enumerate(chosen):
            for j in range(halves):
                cols = pl.ds(column(index_ref, ring_size, half, blocks[k], j), half)
                cut = slice((m * halves + j) * half, (m * halves + j + 1) * half)
                out_ref[0, 0, :, cols] = ins[:hidden_units, cut]
                out_ref[0, 1, :, cols] = ins[hidden_units:, cut]
                out_ref[0, 2, :, cols] = outs[:, cut]


def device_step(tokens, cotangent, routes, gates, expert_weights):
    groups = lax.axis_size("expert")
    ring_size = lax.axis_size("ring")
    slots = groups * CAP
    width = tokens.shape[1]
    send = pl.pallas_call(
        pack_kernel, out_shape=jax.ShapeDtypeStruct((2, slots, 2 * width), BF16)
    )(routes.T, gates.T, tokens, cotangent)
    around = [
        (z * 2 + c, ((z + 1 - 2 * c) % ring_size) * 2 + c)
        for z in range(ring_size)
        for c in range(2)
    ]

    def swapped(x):
        return lax.ppermute(x, "core", [(0, 1), (1, 0)])

    own = lax.all_to_all(
        send.reshape(2 * groups, CAP, 2 * width),
        ("half", "expert"),
        split_axis=0,
        concat_axis=0,
        tiled=True,
    ).reshape(2, slots, 2 * width)
    far = ring_size // 2
    held = {(0, 0, 0): own, (0, 1, 0): swapped(own)}
    raw = {}
    for step in range(1, far + 1):
        for chain in range(2 if step < far else 1):
            piece = lax.ppermute(held[step - 1, chain, 0], ("ring", "core"), around)
            raw[step, chain, 0] = piece
            if step > 1:
                crossed = swapped(held[step - 1, chain, 0])
                raw[step - 1, chain, 1] = crossed
                piece, crossed = lax.optimization_barrier((piece, crossed))
                held[step - 1, chain, 1] = crossed
            held[step, chain, 0] = piece
    held[far - 1, 1, 1] = swapped(held[far - 1, 1, 0])
    held[far, 0, 1] = swapped(held[far, 0, 0])
    blocks = list(held)
    index = jnp.stack([lax.axis_index("ring"), lax.axis_index("core")]).astype(jnp.int32)
    hidden_units = expert_weights.shape[2]
    features = expert_weights.shape[3]
    any_spec = pl.BlockSpec(memory_space=pl.ANY)
    smem_spec = pl.BlockSpec(memory_space=pltpu.SMEM)
    piece_bytes = 8 * slots * width
    weight_bytes = 6 * hidden_units * features
    block_flops = 12 * slots * width * hidden_units
    early = {
        "early_0": [(0, 0, 0), (0, 1, 0)],
        "early_1": [(1, c, t) for t in range(2) for c in range(2)],
        "early_2": [(s, c, t) for s in range(2, far - 1) for t in range(2) for c in range(2)],
        "early_3": [(far - 1, 0, 0), (far - 1, 0, 1), (far - 1, 1, 0)],
        "early_4": [(far - 1, 1, 1), (far, 0, 0)],
    }
    late = [(far, 0, 1)]
    sums = jax.ShapeDtypeStruct((slots, 3 * hidden_units), F32)

    def weight_scratch(count):
        return pltpu.VMEM((count, 2, 3, hidden_units, width), BF16)

    partials = []
    for chosen in early.values():
        chained = len(partials)
        partials = [
            pl.pallas_call(
                functools.partial(forward_kernel, ring_size, chosen, chained),
                out_shape=sums,
                in_specs=[smem_spec, any_spec] + [any_spec] * (chained + len(chosen)),
                out_specs=pl.BlockSpec(memory_space=pltpu.VMEM),
                scratch_shapes=[
                    pltpu.VMEM((len(chosen), 2, slots, 2 * width), BF16),
                    weight_scratch(len(chosen)),
                    pltpu.SemaphoreType.DMA((chained + 3 * len(chosen),)),
                ],
                cost_estimate=pl.CostEstimate(
                    flops=len(chosen) * block_flops,
                    bytes_accessed=len(chosen) * piece_bytes,
                    transcendentals=0,
                ),
                compiler_params=pltpu.CompilerParams(vmem_limit_bytes=EARLY_VMEM),
            )(index, expert_weights, *partials, *[raw.get(k, held[k]) for k in chosen])
        ]
    return pl.pallas_call(
        functools.partial(grads_kernel, ring_size, blocks, late),
        out_shape=jax.ShapeDtypeStruct(expert_weights.shape, BF16),
        in_specs=[smem_spec, any_spec, any_spec] + [any_spec] * len(blocks),
        out_specs=pl.BlockSpec(memory_space=pltpu.VMEM),
        scratch_shapes=[
            pltpu.VMEM((len(blocks), 2, slots, 2 * width), BF16),
            weight_scratch(len(late)),
            pltpu.VMEM(sums.shape, F32),
            pltpu.SemaphoreType.DMA((1 + 2 * len(late) + len(blocks),)),
        ],
        cost_estimate=pl.CostEstimate(
            flops=len(blocks) * block_flops,
            bytes_accessed=len(blocks) * piece_bytes + weight_bytes,
            transcendentals=slots * hidden_units,
        ),
        compiler_params=pltpu.CompilerParams(vmem_limit_bytes=GRADS_VMEM),
    )(index, expert_weights, *partials, *[held[k] for k in blocks])


def solution(mesh):
    sizes = dict(zip(mesh.axis_names, mesh.devices.shape))
    fine = Mesh(
        mesh.devices.reshape(2, sizes["dp"] // 4, 2, sizes["expert"]),
        ("half", "ring", "core", "expert"),
    )
    dp = ("half", "ring", "core")
    return jax.shard_map(
        device_step,
        mesh=fine,
        in_specs=(
            P("expert", dp),
            P("expert", dp),
            P("expert", None),
            P("expert", None),
            P("expert", None, dp, None),
        ),
        out_specs=P("expert", None, dp, None),
        check_vma=False,
    )
```

```python
import functools

import jax
import jax.numpy as jnp
from jax import lax
from jax.experimental import pallas as pl
from jax.experimental.pallas import tpu as pltpu
from jax.sharding import Mesh
from jax.sharding import PartitionSpec as P

CAP = 40
BF16 = jnp.bfloat16
F32 = jnp.float32
EARLY_VMEM = 8 << 20
GRADS_VMEM = 16 << 20
FORWARD_GROUP = 4
GRADS_GROUP = 2


def pack_kernel(routes_ref, gates_ref, tokens_ref, cotangent_ref, out_ref):
    tokens = routes_ref.shape[1]
    copies, slots, width = out_ref.shape
    experts = slots // CAP
    ids = lax.broadcasted_iota(jnp.int32, (experts, tokens), 0)
    named = jnp.zeros((experts, tokens), F32)
    weight = jnp.zeros((experts, tokens), F32)
    for k in range(routes_ref.shape[0]):
        hit = routes_ref[k : k + 1, :] == ids
        named = named + jnp.where(hit, 1.0, 0.0)
        weight = weight + jnp.where(hit, gates_ref[k : k + 1, :], 0.0)
    down = lax.broadcasted_iota(jnp.int32, (tokens, tokens), 0)
    across = lax.broadcasted_iota(jnp.int32, (tokens, tokens), 1)
    before = jnp.where(down < across, 1.0, 0.0).astype(BF16)
    earlier = jnp.dot(named.astype(BF16), before, preferred_element_type=F32)
    place = jnp.where(named > 0.0, earlier, -1.0)
    places = lax.broadcasted_iota(jnp.int32, (CAP, tokens), 0).astype(F32)
    select, weights = [], []
    for e in range(experts):
        hit = place[e : e + 1, :] == places
        select.append(jnp.where(hit, 1.0, 0.0))
        weights.append(jnp.sum(jnp.where(hit, weight[e : e + 1, :], 0.0), axis=1, keepdims=True))
    select = jnp.concatenate(select, axis=0).astype(BF16)
    weights = jnp.concatenate(weights, axis=0)
    rows = jnp.dot(select, tokens_ref[...], preferred_element_type=F32).astype(BF16)
    scaled = jnp.dot(select, cotangent_ref[...], preferred_element_type=F32)
    scaled = (scaled * weights).astype(BF16)
    for j in range(copies):
        out_ref[j, :, : width // 2] = rows
        out_ref[j, :, width // 2 :] = scaled


def column(index_ref, ring_size, half, block, j):
    step, chain, turned = block
    ring, core = index_ref[0], index_ref[1]
    way = (1 - 2 * core) * (1 - 2 * turned)
    z = lax.rem(ring - way * step + 2 * ring_size, ring_size)
    other = chain ^ turned
    c = core + other - 2 * core * other
    return pl.multiple_of(((j * ring_size + z) * 2 + c) * half, half)


def joined(pieces, part):
    half = pieces[0].shape[2] // 2
    cut = slice(part * half, (part + 1) * half)
    return jnp.concatenate(
        [piece[j, :, cut] for piece in pieces for j in range(piece.shape[0])], axis=1
    )


def add_forward(ring_size, index_ref, weights_ref, total, pieces, blocks):
    halves, half = pieces[0].shape[0], pieces[0].shape[2] // 2
    hidden_units = weights_ref.shape[2]
    along = (((1,), (1,)), ((), ()))

    def weight_block(m):
        return jnp.concatenate(
            [
                weights_ref[0, m, :, pl.ds(column(index_ref, ring_size, half, block, j), half)]
                for block in blocks
                for j in range(halves)
            ],
            axis=1,
        )

    pair = jnp.concatenate([weight_block(0), weight_block(1)], axis=0)
    total[:, : 2 * hidden_units] += lax.dot_general(
        joined(pieces, 0), pair, along, preferred_element_type=F32
    )
    total[:, 2 * hidden_units :] += lax.dot_general(
        joined(pieces, 1), weight_block(2), along, preferred_element_type=F32
    )


def forward_kernel(ring_size, blocks, chained, index_ref, weights_ref, *refs):
    count = len(blocks)
    partials, sources, total = refs[:chained], refs[chained : chained + count], refs[chained + count]
    total[...] = partials[0][...] if chained else jnp.zeros_like(total)
    for k in range(0, count, FORWARD_GROUP):
        chosen = range(k, min(k + FORWARD_GROUP, count))
        add_forward(
            ring_size, index_ref, weights_ref, total,
            [sources[n] for n in chosen], [blocks[n] for n in chosen],
        )


def grads_kernel(ring_size, blocks, late, index_ref, weights_ref, partial_ref, *refs):
    count = len(blocks)
    sources, out_ref, total = refs[:count], refs[count], refs[count + 1]
    halves, half = sources[0].shape[0], sources[0].shape[2] // 2
    hidden_units = weights_ref.shape[2]
    last = [blocks.index(block) for block in late]
    total[...] = partial_ref[...]
    add_forward(ring_size, index_ref, weights_ref, total, [sources[k] for k in last], late)
    gate_part = total[:, :hidden_units]
    up_part = total[:, hidden_units : 2 * hidden_units]
    back_hidden = total[:, 2 * hidden_units :]
    sigmoid_part = jax.nn.sigmoid(gate_part)
    silu = gate_part * sigmoid_part
    hidden = (silu * up_part).astype(BF16)
    derivative = sigmoid_part * (1.0 + gate_part * (1.0 - sigmoid_part))
    pre_gate = (back_hidden * up_part * derivative).astype(BF16)
    pre_up = (back_hidden * silu).astype(BF16)
    both = jnp.concatenate([pre_gate, pre_up], axis=1).T
    hidden_t = hidden.T
    for n in range(0, count, GRADS_GROUP):
        chosen = range(n, min(n + GRADS_GROUP, count))
        pieces = [sources[k] for k in chosen]
        ins = jnp.dot(both, joined(pieces, 0), preferred_element_type=F32).astype(BF16)
        outs = jnp.dot(hidden_t, joined(pieces, 1), preferred_element_type=F32).astype(BF16)
        for m, k in enumerate(chosen):
            for j in range(halves):
                cols = pl.ds(column(index_ref, ring_size, half, blocks[k], j), half)
                cut = slice((m * halves + j) * half, (m * halves + j + 1) * half)
                out_ref[0, 0, :, cols] = ins[:hidden_units, cut]
                out_ref[0, 1, :, cols] = ins[hidden_units:, cut]
                out_ref[0, 2, :, cols] = outs[:, cut]


def device_step(tokens, cotangent, routes, gates, expert_weights):
    groups = lax.axis_size("expert")
    ring_size = lax.axis_size("ring")
    slots = groups * CAP
    width = tokens.shape[1]
    send = pl.pallas_call(
        pack_kernel, out_shape=jax.ShapeDtypeStruct((2, slots, 2 * width), BF16)
    )(routes.T, gates.T, tokens, cotangent)
    around = [
        (z * 2 + c, ((z + 1 - 2 * c) % ring_size) * 2 + c)
        for z in range(ring_size)
        for c in range(2)
    ]

    def swapped(x):
        return lax.ppermute(x, "core", [(0, 1), (1, 0)])

    own = lax.all_to_all(
        send.reshape(2 * groups, CAP, 2 * width),
        ("half", "expert"),
        split_axis=0,
        concat_axis=0,
        tiled=True,
    ).reshape(2, slots, 2 * width)
    far = ring_size // 2
    held = {(0, 0, 0): own, (0, 1, 0): swapped(own)}
    raw = {}
    for step in range(1, far + 1):
        for chain in range(2 if step < far else 1):
            piece = lax.ppermute(held[step - 1, chain, 0], ("ring", "core"), around)
            raw[step, chain, 0] = piece
            if step > 1:
                crossed = swapped(held[step - 1, chain, 0])
                raw[step - 1, chain, 1] = crossed
                piece, crossed = lax.optimization_barrier((piece, crossed))
                held[step - 1, chain, 1] = crossed
            held[step, chain, 0] = piece
    held[far - 1, 1, 1] = swapped(held[far - 1, 1, 0])
    held[far, 0, 1] = swapped(held[far, 0, 0])
    blocks = list(held)
    index = jnp.stack([lax.axis_index("ring"), lax.axis_index("core")]).astype(jnp.int32)
    hidden_units = expert_weights.shape[2]
    features = expert_weights.shape[3]
    vmem_spec = pl.BlockSpec(memory_space=pltpu.VMEM)
    smem_spec = pl.BlockSpec(memory_space=pltpu.SMEM)
    piece_bytes = 8 * slots * width
    weight_bytes = 6 * hidden_units * features
    block_flops = 12 * slots * width * hidden_units
    early = {
        "early_0": [(0, 0, 0), (0, 1, 0)],
        "early_1": [(1, c, t) for t in range(2) for c in range(2)],
        "early_2": [(s, c, t) for s in range(2, far - 1) for t in range(2) for c in range(2)],
        "early_3": [(far - 1, 0, 0), (far - 1, 0, 1), (far - 1, 1, 0)],
        "early_4": [(far - 1, 1, 1), (far, 0, 0)],
    }
    late = [(far, 0, 1)]
    sums = jax.ShapeDtypeStruct((slots, 3 * hidden_units), F32)

    partials = []
    for chosen in early.values():
        chained = len(partials)
        partials = [
            pl.pallas_call(
                functools.partial(forward_kernel, ring_size, chosen, chained),
                out_shape=sums,
                in_specs=[smem_spec, vmem_spec] + [vmem_spec] * (chained + len(chosen)),
                out_specs=pl.BlockSpec(memory_space=pltpu.VMEM),
                cost_estimate=pl.CostEstimate(
                    flops=len(chosen) * block_flops,
                    bytes_accessed=len(chosen) * piece_bytes,
                    transcendentals=0,
                ),
                compiler_params=pltpu.CompilerParams(vmem_limit_bytes=EARLY_VMEM),
            )(index, expert_weights, *partials, *[raw.get(k, held[k]) for k in chosen])
        ]
    return pl.pallas_call(
        functools.partial(grads_kernel, ring_size, blocks, late),
        out_shape=jax.ShapeDtypeStruct(expert_weights.shape, BF16),
        in_specs=[smem_spec, vmem_spec, vmem_spec] + [vmem_spec] * len(blocks),
        out_specs=pl.BlockSpec(memory_space=pltpu.VMEM),
        scratch_shapes=[pltpu.VMEM(sums.shape, F32)],
        cost_estimate=pl.CostEstimate(
            flops=len(blocks) * block_flops,
            bytes_accessed=len(blocks) * piece_bytes + weight_bytes,
            transcendentals=slots * hidden_units,
        ),
        compiler_params=pltpu.CompilerParams(vmem_limit_bytes=GRADS_VMEM),
    )(index, expert_weights, *partials, *[held[k] for k in blocks])


def solution(mesh):
    sizes = dict(zip(mesh.axis_names, mesh.devices.shape))
    fine = Mesh(
        mesh.devices.reshape(2, sizes["dp"] // 4, 2, sizes["expert"]),
        ("half", "ring", "core", "expert"),
    )
    dp = ("half", "ring", "core")
    return jax.shard_map(
        device_step,
        mesh=fine,
        in_specs=(
            P("expert", dp),
            P("expert", dp),
            P("expert", None),
            P("expert", None),
            P("expert", None, dp, None),
        ),
        out_specs=P("expert", None, dp, None),
        check_vma=False,
    )
```

```python
import functools

import jax
import jax.numpy as jnp
from jax import lax
from jax.experimental import pallas as pl
from jax.experimental.pallas import tpu as pltpu
from jax.sharding import Mesh
from jax.sharding import PartitionSpec as P

CAP = 40
BF16 = jnp.bfloat16
F32 = jnp.float32
EARLY_VMEM = 8 << 20
GRADS_VMEM = 16 << 20
FORWARD_GROUP = 4
GRADS_GROUP = 2


def pack_kernel(routes_ref, gates_ref, tokens_ref, cotangent_ref, out_ref):
    tokens = routes_ref.shape[1]
    copies, slots, width = out_ref.shape
    experts = slots // CAP
    ids = lax.broadcasted_iota(jnp.int32, (experts, tokens), 0)
    named = jnp.zeros((experts, tokens), F32)
    weight = jnp.zeros((experts, tokens), F32)
    for k in range(routes_ref.shape[0]):
        hit = routes_ref[k : k + 1, :] == ids
        named = named + jnp.where(hit, 1.0, 0.0)
        weight = weight + jnp.where(hit, gates_ref[k : k + 1, :], 0.0)
    down = lax.broadcasted_iota(jnp.int32, (tokens, tokens), 0)
    across = lax.broadcasted_iota(jnp.int32, (tokens, tokens), 1)
    before = jnp.where(down < across, 1.0, 0.0).astype(BF16)
    earlier = jnp.dot(named.astype(BF16), before, preferred_element_type=F32)
    place = jnp.where(named > 0.0, earlier, -1.0)
    places = lax.broadcasted_iota(jnp.int32, (CAP, tokens), 0).astype(F32)
    select, weights = [], []
    for e in range(experts):
        hit = place[e : e + 1, :] == places
        select.append(jnp.where(hit, 1.0, 0.0))
        weights.append(jnp.sum(jnp.where(hit, weight[e : e + 1, :], 0.0), axis=1, keepdims=True))
    select = jnp.concatenate(select, axis=0).astype(BF16)
    weights = jnp.concatenate(weights, axis=0)
    rows = jnp.dot(select, tokens_ref[...], preferred_element_type=F32).astype(BF16)
    scaled = jnp.dot(select, cotangent_ref[...], preferred_element_type=F32)
    scaled = (scaled * weights).astype(BF16)
    for j in range(copies):
        out_ref[j, :, : width // 2] = rows
        out_ref[j, :, width // 2 :] = scaled


def column(index_ref, ring_size, half, block, j):
    step, chain, turned = block
    ring, core = index_ref[0], index_ref[1]
    way = (1 - 2 * core) * (1 - 2 * turned)
    z = lax.rem(ring - way * step + 2 * ring_size, ring_size)
    other = chain ^ turned
    c = core + other - 2 * core * other
    return pl.multiple_of(((j * ring_size + z) * 2 + c) * half, half)


def joined(pieces, part):
    half = pieces[0].shape[2] // 2
    cut = slice(part * half, (part + 1) * half)
    return jnp.concatenate(
        [piece[j, :, cut] for piece in pieces for j in range(piece.shape[0])], axis=1
    )


def add_forward(ring_size, index_ref, weights_ref, total, pieces, blocks):
    halves, half = pieces[0].shape[0], pieces[0].shape[2] // 2
    hidden_units = weights_ref.shape[2]
    along = (((1,), (1,)), ((), ()))

    def weight_block(m):
        return jnp.concatenate(
            [
                weights_ref[0, m, :, pl.ds(column(index_ref, ring_size, half, block, j), half)]
                for block in blocks
                for j in range(halves)
            ],
            axis=1,
        )

    pair = jnp.concatenate([weight_block(0), weight_block(1)], axis=0)
    total[:, : 2 * hidden_units] += lax.dot_general(
        joined(pieces, 0), pair, along, preferred_element_type=F32
    )
    total[:, 2 * hidden_units :] += lax.dot_general(
        joined(pieces, 1), weight_block(2), along, preferred_element_type=F32
    )


def forward_kernel(ring_size, blocks, chained, index_ref, weights_ref, *refs):
    count = len(blocks)
    partials, sources, total = refs[:chained], refs[chained : chained + count], refs[chained + count]
    total[...] = partials[0][...] if chained else jnp.zeros_like(total)
    for k in range(0, count, FORWARD_GROUP):
        chosen = range(k, min(k + FORWARD_GROUP, count))
        add_forward(
            ring_size, index_ref, weights_ref, total,
            [sources[n] for n in chosen], [blocks[n] for n in chosen],
        )


def grads_kernel(ring_size, blocks, late, index_ref, weights_ref, partial_ref, *refs):
    count = len(blocks)
    sources, out_ref = refs[:count], refs[count]
    total, out_buf, sems = refs[count + 1 :]
    halves, half = sources[0].shape[0], sources[0].shape[2] // 2
    hidden_units = weights_ref.shape[2]
    last = [blocks.index(block) for block in late]
    total[...] = partial_ref[...]
    add_forward(ring_size, index_ref, weights_ref, total, [sources[k] for k in last], late)
    gate_part = total[:, :hidden_units]
    up_part = total[:, hidden_units : 2 * hidden_units]
    back_hidden = total[:, 2 * hidden_units :]
    sigmoid_part = jax.nn.sigmoid(gate_part)
    silu = gate_part * sigmoid_part
    hidden = (silu * up_part).astype(BF16)
    derivative = sigmoid_part * (1.0 + gate_part * (1.0 - sigmoid_part))
    pre_gate = (back_hidden * up_part * derivative).astype(BF16)
    pre_up = (back_hidden * silu).astype(BF16)
    both = jnp.concatenate([pre_gate, pre_up], axis=1).T
    hidden_t = hidden.T
    copies = []
    for n in range(0, count, GRADS_GROUP):
        chosen = range(n, min(n + GRADS_GROUP, count))
        pieces = [sources[k] for k in chosen]
        ins = jnp.dot(both, joined(pieces, 0), preferred_element_type=F32).astype(BF16)
        outs = jnp.dot(hidden_t, joined(pieces, 1), preferred_element_type=F32).astype(BF16)
        for m, k in enumerate(chosen):
            for j in range(halves):
                cut = slice((m * halves + j) * half, (m * halves + j + 1) * half)
                out_buf[k, j, 0] = ins[:hidden_units, cut]
                out_buf[k, j, 1] = ins[hidden_units:, cut]
                out_buf[k, j, 2] = outs[:, cut]
                cols = pl.ds(column(index_ref, ring_size, half, blocks[k], j), half)
                copy = pltpu.make_async_copy(
                    out_buf.at[k, j], out_ref.at[0, :, :, cols], sems.at[k, j]
                )
                copy.start()
                copies.append(copy)
    for copy in copies:
        copy.wait()


def device_step(tokens, cotangent, routes, gates, expert_weights):
    groups = lax.axis_size("expert")
    ring_size = lax.axis_size("ring")
    slots = groups * CAP
    width = tokens.shape[1]
    send = pl.pallas_call(
        pack_kernel,
        out_shape=jax.ShapeDtypeStruct((2, slots, 2 * width), BF16),
    )(routes.T, gates.T, tokens, cotangent)
    around = [
        (z * 2 + c, ((z + 1 - 2 * c) % ring_size) * 2 + c)
        for z in range(ring_size)
        for c in range(2)
    ]

    def swapped(x):
        return lax.ppermute(x, "core", [(0, 1), (1, 0)])

    own = lax.all_to_all(
        send.reshape(2 * groups, CAP, 2 * width),
        ("half", "expert"),
        split_axis=0,
        concat_axis=0,
        tiled=True,
    ).reshape(2, slots, 2 * width)
    far = ring_size // 2
    held = {(0, 0, 0): own, (0, 1, 0): swapped(own)}
    raw = {}
    for step in range(1, far + 1):
        for chain in range(2 if step < far else 1):
            piece = lax.ppermute(held[step - 1, chain, 0], ("ring", "core"), around)
            raw[step, chain, 0] = piece
            if step > 1:
                crossed = swapped(held[step - 1, chain, 0])
                raw[step - 1, chain, 1] = crossed
                piece, crossed = lax.optimization_barrier((piece, crossed))
                held[step - 1, chain, 1] = crossed
            held[step, chain, 0] = piece
    held[far - 1, 1, 1] = swapped(held[far - 1, 1, 0])
    held[far, 0, 1] = swapped(held[far, 0, 0])
    blocks = list(held)
    index = jnp.stack([lax.axis_index("ring"), lax.axis_index("core")]).astype(jnp.int32)
    hidden_units = expert_weights.shape[2]
    features = expert_weights.shape[3]
    vmem_spec = pl.BlockSpec(memory_space=pltpu.VMEM)
    smem_spec = pl.BlockSpec(memory_space=pltpu.SMEM)
    piece_bytes = 8 * slots * width
    weight_bytes = 6 * hidden_units * features
    block_flops = 12 * slots * width * hidden_units
    early = {
        "early_0": [(0, 0, 0), (0, 1, 0)],
        "early_1": [(1, c, t) for t in range(2) for c in range(2)],
        "early_2": [(s, c, t) for s in range(2, far - 1) for t in range(2) for c in range(2)],
        "early_3": [(far - 1, 0, 0), (far - 1, 0, 1), (far - 1, 1, 0)],
        "early_4": [(far - 1, 1, 1), (far, 0, 0)],
    }
    late = [(far, 0, 1)]
    sums = jax.ShapeDtypeStruct((slots, 3 * hidden_units), F32)

    partials = []
    for chosen in early.values():
        chained = len(partials)
        partials = [
            pl.pallas_call(
                functools.partial(forward_kernel, ring_size, chosen, chained),
                out_shape=sums,
                in_specs=[smem_spec, vmem_spec] + [vmem_spec] * (chained + len(chosen)),
                out_specs=pl.BlockSpec(memory_space=pltpu.VMEM),
                cost_estimate=pl.CostEstimate(
                    flops=len(chosen) * block_flops,
                    bytes_accessed=len(chosen) * piece_bytes,
                    transcendentals=0,
                ),
                compiler_params=pltpu.CompilerParams(vmem_limit_bytes=EARLY_VMEM),
            )(index, expert_weights, *partials, *[raw.get(k, held[k]) for k in chosen])
        ]
    return pl.pallas_call(
        functools.partial(grads_kernel, ring_size, blocks, late),
        out_shape=jax.ShapeDtypeStruct(expert_weights.shape, BF16),
        in_specs=[smem_spec, vmem_spec, vmem_spec] + [vmem_spec] * len(blocks),
        out_specs=pl.BlockSpec(memory_space=pl.ANY),
        scratch_shapes=[
            pltpu.VMEM(sums.shape, F32),
            pltpu.VMEM((len(blocks), 2, 3, hidden_units, width), BF16),
            pltpu.SemaphoreType.DMA((len(blocks), 2)),
        ],
        cost_estimate=pl.CostEstimate(
            flops=len(blocks) * block_flops,
            bytes_accessed=len(blocks) * piece_bytes + weight_bytes,
            transcendentals=slots * hidden_units,
        ),
        compiler_params=pltpu.CompilerParams(vmem_limit_bytes=GRADS_VMEM),
    )(index, expert_weights, *partials, *[held[k] for k in blocks])


def solution(mesh):
    sizes = dict(zip(mesh.axis_names, mesh.devices.shape))
    fine = Mesh(
        mesh.devices.reshape(2, sizes["dp"] // 4, 2, sizes["expert"]),
        ("half", "ring", "core", "expert"),
    )
    dp = ("half", "ring", "core")
    return jax.shard_map(
        device_step,
        mesh=fine,
        in_specs=(
            P("expert", dp),
            P("expert", dp),
            P("expert", None),
            P("expert", None),
            P("expert", None, dp, None),
        ),
        out_specs=P("expert", None, dp, None),
        check_vma=False,
    )
```

```python
import functools

import jax
import jax.numpy as jnp
from jax import lax
from jax.experimental import pallas as pl
from jax.experimental.pallas import tpu as pltpu
from jax.sharding import Mesh
from jax.sharding import PartitionSpec as P

CAP = 40
BF16 = jnp.bfloat16
F32 = jnp.float32
EARLY_VMEM = 8 << 20
GRADS_VMEM = 16 << 20
FORWARD_GROUP = 2
GRADS_GROUP = 2


def pack_kernel(routes_in, gates_in, tokens_in, cotangent_in, out_ref, *scratch):
    routes_ref, gates_ref, tokens_ref, cotangent_ref, packed, in_sems, out_sems = scratch
    loads = []
    for n, (source, place) in enumerate(
        (
            (routes_in, routes_ref),
            (gates_in, gates_ref),
            (tokens_in, tokens_ref),
            (cotangent_in, cotangent_ref),
        )
    ):
        load = pltpu.make_async_copy(source, place, in_sems.at[n])
        load.start()
        loads.append(load)
    tokens = routes_ref.shape[1]
    copies, slots, width = out_ref.shape
    for load in loads:
        load.wait()
    experts = slots // CAP
    ids = lax.broadcasted_iota(jnp.int32, (experts, tokens), 0)
    named = jnp.zeros((experts, tokens), F32)
    weight = jnp.zeros((experts, tokens), F32)
    for k in range(routes_ref.shape[0]):
        hit = routes_ref[k : k + 1, :] == ids
        named = named + jnp.where(hit, 1.0, 0.0)
        weight = weight + jnp.where(hit, gates_ref[k : k + 1, :], 0.0)
    down = lax.broadcasted_iota(jnp.int32, (tokens, tokens), 0)
    across = lax.broadcasted_iota(jnp.int32, (tokens, tokens), 1)
    before = jnp.where(down < across, 1.0, 0.0).astype(BF16)
    earlier = jnp.dot(named.astype(BF16), before, preferred_element_type=F32)
    place = jnp.where(named > 0.0, earlier, -1.0)
    places = lax.broadcasted_iota(jnp.int32, (CAP, tokens), 0).astype(F32)
    select, weights = [], []
    for e in range(experts):
        hit = place[e : e + 1, :] == places
        select.append(jnp.where(hit, 1.0, 0.0))
        weights.append(jnp.sum(jnp.where(hit, weight[e : e + 1, :], 0.0), axis=1, keepdims=True))
    select = jnp.concatenate(select, axis=0).astype(BF16)
    weights = jnp.concatenate(weights, axis=0)
    half = width // 2
    stores = []

    def store(part):
        for j in range(copies):
            copy = pltpu.make_async_copy(
                packed.at[part], out_ref.at[j, :, pl.ds(part * half, half)], out_sems.at[part, j]
            )
            copy.start()
            stores.append(copy)

    rows = jnp.dot(select, tokens_ref[...], preferred_element_type=F32)
    packed[0] = rows.astype(BF16)
    store(0)
    scaled = jnp.dot(select, cotangent_ref[...], preferred_element_type=F32)
    packed[1] = (scaled * weights).astype(BF16)
    store(1)
    for copy in stores:
        copy.wait()


def column(index_ref, ring_size, half, block, j):
    step, chain, turned, sides = block
    ring, core = index_ref[0], index_ref[1]
    way = (1 - 2 * core) * (1 - 2 * turned)
    z = lax.rem(ring - way * step + 2 * ring_size, ring_size)
    other = chain ^ turned
    c = core + other - 2 * core * other
    return pl.multiple_of(((sides[j] * ring_size + z) * 2 + c) * half, half)


def joined(pieces, part):
    half = pieces[0].shape[2] // 2
    cut = slice(part * half, (part + 1) * half)
    return jnp.concatenate(
        [piece[j, :, cut] for piece in pieces for j in range(piece.shape[0])], axis=1
    )


def add_forward(ring_size, index_ref, weights_ref, total, pieces, blocks):
    half = pieces[0].shape[2] // 2
    along = (((1,), (1,)), ((), ()))

    def weight_block(m):
        return jnp.concatenate(
            [
                weights_ref[0, m, :, pl.ds(column(index_ref, ring_size, half, block, j), half)]
                for block in blocks
                for j in range(len(block[3]))
            ],
            axis=1,
        )

    hidden_units = weights_ref.shape[2]
    pair = jnp.concatenate([weight_block(0), weight_block(1)], axis=0)
    total[: 2 * hidden_units] += lax.dot_general(
        pair, joined(pieces, 0), along, preferred_element_type=F32
    )
    total[2 * hidden_units :] += lax.dot_general(
        weight_block(2), joined(pieces, 1), along, preferred_element_type=F32
    )


def forward_kernel(ring_size, blocks, chained, index_ref, weights_ref, *refs):
    count = len(blocks)
    partials, sources, total = refs[:chained], refs[chained : chained + count], refs[chained + count]
    total[...] = partials[0][...] if chained else jnp.zeros_like(total)
    for k in range(0, count, FORWARD_GROUP):
        chosen = range(k, min(k + FORWARD_GROUP, count))
        add_forward(
            ring_size, index_ref, weights_ref, total,
            [sources[n] for n in chosen], [blocks[n] for n in chosen],
        )


def grads_kernel(ring_size, blocks, late, index_ref, weights_ref, partial_ref, *refs):
    count = len(blocks)
    sources, out_ref = refs[:count], refs[count]
    total, out_buf, sems = refs[count + 1 :]
    half = sources[0].shape[2] // 2
    hidden_units = weights_ref.shape[2]
    last = [blocks.index(block) for block in late]
    total[...] = partial_ref[...]
    add_forward(ring_size, index_ref, weights_ref, total, [sources[k] for k in last], late)
    gate_part = total[:hidden_units]
    up_part = total[hidden_units : 2 * hidden_units]
    back_hidden = total[2 * hidden_units :]
    sigmoid_part = jax.nn.sigmoid(gate_part)
    silu = gate_part * sigmoid_part
    hidden = (silu * up_part).astype(BF16)
    derivative = sigmoid_part * (1.0 + gate_part * (1.0 - sigmoid_part))
    pre_gate = (back_hidden * up_part * derivative).astype(BF16)
    pre_up = (back_hidden * silu).astype(BF16)
    both = jnp.concatenate([pre_gate, pre_up], axis=0)
    copies = []
    for n in range(0, count, GRADS_GROUP):
        chosen = range(n, min(n + GRADS_GROUP, count))
        pieces = [sources[k] for k in chosen]
        ins = jnp.dot(both, joined(pieces, 0), preferred_element_type=F32).astype(BF16)
        outs = jnp.dot(hidden, joined(pieces, 1), preferred_element_type=F32).astype(BF16)
        at = 0
        for k in chosen:
            for j in range(len(blocks[k][3])):
                cut = slice(at, at + half)
                at += half
                out_buf[k, j, 0] = ins[:hidden_units, cut]
                out_buf[k, j, 1] = ins[hidden_units:, cut]
                out_buf[k, j, 2] = outs[:, cut]
                cols = pl.ds(column(index_ref, ring_size, half, blocks[k], j), half)
                copy = pltpu.make_async_copy(
                    out_buf.at[k, j], out_ref.at[0, :, :, cols], sems.at[k, j]
                )
                copy.start()
                copies.append(copy)
    for copy in copies:
        copy.wait()


def device_step(tokens, cotangent, routes, gates, expert_weights):
    groups = lax.axis_size("expert")
    ring_size = lax.axis_size("ring")
    slots = groups * CAP
    width = tokens.shape[1]
    send = pl.pallas_call(
        pack_kernel,
        out_shape=jax.ShapeDtypeStruct((2, slots, 2 * width), BF16),
        in_specs=[pl.BlockSpec(memory_space=pl.ANY)] * 4,
        out_specs=pl.BlockSpec(memory_space=pl.ANY),
        scratch_shapes=[
            pltpu.VMEM(routes.shape[::-1], routes.dtype),
            pltpu.VMEM(gates.shape[::-1], F32),
            pltpu.VMEM(tokens.shape, BF16),
            pltpu.VMEM(cotangent.shape, BF16),
            pltpu.VMEM((2, slots, width), BF16),
            pltpu.SemaphoreType.DMA((4,)),
            pltpu.SemaphoreType.DMA((2, 2)),
        ],
    )(routes.T, gates.T, tokens, cotangent)
    around = [
        (z * 2 + c, ((z + 1 - 2 * c) % ring_size) * 2 + c)
        for z in range(ring_size)
        for c in range(2)
    ]

    def swapped(x):
        return lax.ppermute(x, "core", [(0, 1), (1, 0)])

    own = lax.all_to_all(
        send.reshape(2 * groups, CAP, 2 * width),
        ("half", "expert"),
        split_axis=0,
        concat_axis=0,
        tiled=True,
    ).reshape(2, slots, 2 * width)
    far = ring_size // 2
    both = (0, 1)
    held = {(0, 0, 0, both): own, (0, 1, 0, both): swapped(own)}
    raw = {}
    ring = ("ring", "core")

    def cross(step, chain, piece):
        key = (step - 1, chain, 1, both)
        raw[key] = swapped(held[step - 1, chain, 0, both])
        piece, held[key] = lax.optimization_barrier((piece, raw[key]))
        return piece

    for step in range(1, far):
        for chain in range(2):
            piece = lax.ppermute(held[step - 1, chain, 0, both], ring, around)
            raw[step, chain, 0, both] = piece
            held[step, chain, 0, both] = cross(step, chain, piece) if step > 1 else piece
    for side in both:
        piece = held[far - 1, 0, 0, both][side : side + 1]
        held[far, 0, 0, (side,)] = lax.ppermute(piece, ring, around)
    for chain in range(2):
        held[far - 1, chain, 1, both] = swapped(held[far - 1, chain, 0, both])
    for side in both:
        held[far, 0, 1, (side,)] = swapped(held[far, 0, 0, (side,)])
    blocks = list(held)
    index = jnp.stack([lax.axis_index("ring"), lax.axis_index("core")]).astype(jnp.int32)
    hidden_units = expert_weights.shape[2]
    features = expert_weights.shape[3]
    vmem_spec = pl.BlockSpec(memory_space=pltpu.VMEM)
    smem_spec = pl.BlockSpec(memory_space=pltpu.SMEM)
    piece_bytes = 8 * slots * width
    weight_bytes = 6 * hidden_units * features
    block_flops = 12 * slots * width * hidden_units
    early = {
        "early_0": [(0, 0, 0, both), (0, 1, 0, both)],
        "early_1": [(1, c, t, both) for t in range(2) for c in range(2)],
        "early_2": [(s, c, t, both) for s in range(2, far - 1) for t in range(2) for c in range(2)],
        "early_3": [(far - 1, 0, 0, both), (far - 1, 0, 1, both), (far - 1, 1, 0, both)],
        "early_4": [(far - 1, 1, 1, both), (far, 0, 0, (0,)), (far, 0, 0, (1,)), (far, 0, 1, (0,))],
    }
    late = [(far, 0, 1, (1,))]
    sums = jax.ShapeDtypeStruct((3 * hidden_units, slots), F32)

    partials = []
    for chosen in early.values():
        chained = len(partials)
        partials = [
            pl.pallas_call(
                functools.partial(forward_kernel, ring_size, chosen, chained),
                out_shape=sums,
                in_specs=[smem_spec, vmem_spec] + [vmem_spec] * (chained + len(chosen)),
                out_specs=pl.BlockSpec(memory_space=pltpu.VMEM),
                cost_estimate=pl.CostEstimate(
                    flops=len(chosen) * block_flops,
                    bytes_accessed=len(chosen) * piece_bytes,
                    transcendentals=0,
                ),
                compiler_params=pltpu.CompilerParams(vmem_limit_bytes=EARLY_VMEM),
            )(index, expert_weights, *partials, *[raw.get(k, held[k]) for k in chosen])
        ]
    return pl.pallas_call(
        functools.partial(grads_kernel, ring_size, blocks, late),
        out_shape=jax.ShapeDtypeStruct(expert_weights.shape, BF16),
        in_specs=[smem_spec, vmem_spec, vmem_spec] + [vmem_spec] * len(blocks),
        out_specs=pl.BlockSpec(memory_space=pl.ANY),
        scratch_shapes=[
            pltpu.VMEM(sums.shape, F32),
            pltpu.VMEM((len(blocks), 2, 3, hidden_units, width), BF16),
            pltpu.SemaphoreType.DMA((len(blocks), 2)),
        ],
        cost_estimate=pl.CostEstimate(
            flops=len(blocks) * block_flops,
            bytes_accessed=len(blocks) * piece_bytes + weight_bytes,
            transcendentals=slots * hidden_units,
        ),
        compiler_params=pltpu.CompilerParams(vmem_limit_bytes=GRADS_VMEM),
    )(index, expert_weights, *partials, *[held[k] for k in blocks])


def solution(mesh):
    sizes = dict(zip(mesh.axis_names, mesh.devices.shape))
    fine = Mesh(
        mesh.devices.reshape(2, sizes["dp"] // 4, 2, sizes["expert"]),
        ("half", "ring", "core", "expert"),
    )
    dp = ("half", "ring", "core")
    return jax.shard_map(
        device_step,
        mesh=fine,
        in_specs=(
            P("expert", dp),
            P("expert", dp),
            P("expert", None),
            P("expert", None),
            P("expert", None, dp, None),
        ),
        out_specs=P("expert", None, dp, None),
        check_vma=False,
    )
```

```python
import functools

import jax
import jax.numpy as jnp
from jax import lax
from jax.experimental import pallas as pl
from jax.experimental.pallas import tpu as pltpu
from jax.sharding import Mesh
from jax.sharding import PartitionSpec as P

CAP = 40
BF16 = jnp.bfloat16
F32 = jnp.float32
EARLY_VMEM = 8 << 20
GRADS_VMEM = 16 << 20
FORWARD_GROUP = 2
GRADS_GROUP = 2


def pack_kernel(routes_ref, gates_ref, tokens_ref, cotangent_ref, out_ref):
    tokens = routes_ref.shape[1]
    copies, slots, width = out_ref.shape
    experts = slots // CAP
    ids = lax.broadcasted_iota(jnp.int32, (experts, tokens), 0)
    named = jnp.zeros((experts, tokens), F32)
    weight = jnp.zeros((experts, tokens), F32)
    for k in range(routes_ref.shape[0]):
        hit = routes_ref[k : k + 1, :] == ids
        named = named + jnp.where(hit, 1.0, 0.0)
        weight = weight + jnp.where(hit, gates_ref[k : k + 1, :], 0.0)
    down = lax.broadcasted_iota(jnp.int32, (tokens, tokens), 0)
    across = lax.broadcasted_iota(jnp.int32, (tokens, tokens), 1)
    before = jnp.where(down < across, 1.0, 0.0).astype(BF16)
    earlier = jnp.dot(named.astype(BF16), before, preferred_element_type=F32)
    place = jnp.where(named > 0.0, earlier, -1.0)
    places = lax.broadcasted_iota(jnp.int32, (CAP, tokens), 0).astype(F32)
    select, weights = [], []
    for e in range(experts):
        hit = place[e : e + 1, :] == places
        select.append(jnp.where(hit, 1.0, 0.0))
        weights.append(jnp.sum(jnp.where(hit, weight[e : e + 1, :], 0.0), axis=1, keepdims=True))
    select = jnp.concatenate(select, axis=0).astype(BF16)
    weights = jnp.concatenate(weights, axis=0)
    rows = jnp.dot(select, tokens_ref[...], preferred_element_type=F32).astype(BF16)
    scaled = jnp.dot(select, cotangent_ref[...], preferred_element_type=F32)
    scaled = (scaled * weights).astype(BF16)
    for j in range(copies):
        out_ref[j, :, : width // 2] = rows
        out_ref[j, :, width // 2 :] = scaled


def column(index_ref, ring_size, half, block, j):
    step, chain, turned = block
    ring, core = index_ref[0], index_ref[1]
    way = (1 - 2 * core) * (1 - 2 * turned)
    z = lax.rem(ring - way * step + 2 * ring_size, ring_size)
    other = chain ^ turned
    c = core + other - 2 * core * other
    return pl.multiple_of(((j * ring_size + z) * 2 + c) * half, half)


def joined(pieces, part):
    half = pieces[0].shape[2] // 2
    cut = slice(part * half, (part + 1) * half)
    return jnp.concatenate(
        [piece[j, :, cut] for piece in pieces for j in range(piece.shape[0])], axis=1
    )


def add_forward(ring_size, index_ref, weights_ref, total, pieces, blocks):
    halves, half = pieces[0].shape[0], pieces[0].shape[2] // 2
    hidden_units = weights_ref.shape[2]
    along = (((1,), (1,)), ((), ()))

    def weight_block(m):
        return jnp.concatenate(
            [
                weights_ref[0, m, :, pl.ds(column(index_ref, ring_size, half, block, j), half)]
                for block in blocks
                for j in range(halves)
            ],
            axis=1,
        )

    pair = jnp.concatenate([weight_block(0), weight_block(1)], axis=0)
    total[: 2 * hidden_units] += lax.dot_general(
        pair, joined(pieces, 0), along, preferred_element_type=F32
    )
    total[2 * hidden_units :] += lax.dot_general(
        weight_block(2), joined(pieces, 1), along, preferred_element_type=F32
    )


def forward_kernel(ring_size, blocks, chained, index_ref, weights_ref, *refs):
    count = len(blocks)
    partials, sources, total = refs[:chained], refs[chained : chained + count], refs[chained + count]
    total[...] = partials[0][...] if chained else jnp.zeros_like(total)
    for k in range(0, count, FORWARD_GROUP):
        chosen = range(k, min(k + FORWARD_GROUP, count))
        add_forward(
            ring_size, index_ref, weights_ref, total,
            [sources[n] for n in chosen], [blocks[n] for n in chosen],
        )


def grads_kernel(ring_size, blocks, late, moved, index_ref, weights_ref, partial_ref, *refs):
    count = len(blocks)
    sources, out_ref = list(refs[:count]), refs[count]
    total, out_buf, sems, moved_buf, moved_sems = refs[count + 1 :]
    loads = []
    for n, block in enumerate(moved):
        k = blocks.index(block)
        load = pltpu.make_async_copy(sources[k], moved_buf.at[n], moved_sems.at[n])
        load.start()
        loads.append(load)
        sources[k] = moved_buf.at[n]
    halves, half = sources[0].shape[0], sources[0].shape[2] // 2
    hidden_units = weights_ref.shape[2]
    last = [blocks.index(block) for block in late]
    total[...] = partial_ref[...]
    add_forward(ring_size, index_ref, weights_ref, total, [sources[k] for k in last], late)
    for load in loads:
        load.wait()
    gate_part = total[:hidden_units]
    up_part = total[hidden_units : 2 * hidden_units]
    back_hidden = total[2 * hidden_units :]
    sigmoid_part = jax.nn.sigmoid(gate_part)
    silu = gate_part * sigmoid_part
    hidden = (silu * up_part).astype(BF16)
    derivative = sigmoid_part * (1.0 + gate_part * (1.0 - sigmoid_part))
    pre_gate = (back_hidden * up_part * derivative).astype(BF16)
    pre_up = (back_hidden * silu).astype(BF16)
    both = jnp.concatenate([pre_gate, pre_up], axis=0)
    copies = []
    for n in range(0, count, GRADS_GROUP):
        chosen = range(n, min(n + GRADS_GROUP, count))
        pieces = [sources[k] for k in chosen]
        ins = jnp.dot(both, joined(pieces, 0), preferred_element_type=F32).astype(BF16)
        outs = jnp.dot(hidden, joined(pieces, 1), preferred_element_type=F32).astype(BF16)
        for m, k in enumerate(chosen):
            for j in range(halves):
                cut = slice((m * halves + j) * half, (m * halves + j + 1) * half)
                out_buf[k, j, 0] = ins[:hidden_units, cut]
                out_buf[k, j, 1] = ins[hidden_units:, cut]
                out_buf[k, j, 2] = outs[:, cut]
                cols = pl.ds(column(index_ref, ring_size, half, blocks[k], j), half)
                copy = pltpu.make_async_copy(
                    out_buf.at[k, j], out_ref.at[0, :, :, cols], sems.at[k, j]
                )
                copy.start()
                copies.append(copy)
    for copy in copies:
        copy.wait()


def device_step(tokens, cotangent, routes, gates, expert_weights):
    groups = lax.axis_size("expert")
    ring_size = lax.axis_size("ring")
    slots = groups * CAP
    width = tokens.shape[1]
    send = pl.pallas_call(
        pack_kernel,
        out_shape=jax.ShapeDtypeStruct((2, slots, 2 * width), BF16),
    )(routes.T, gates.T, tokens, cotangent)
    around = [
        (z * 2 + c, ((z + 1 - 2 * c) % ring_size) * 2 + c)
        for z in range(ring_size)
        for c in range(2)
    ]

    def swapped(x):
        return lax.ppermute(x, "core", [(0, 1), (1, 0)])

    own = lax.all_to_all(
        send.reshape(2 * groups, CAP, 2 * width),
        ("half", "expert"),
        split_axis=0,
        concat_axis=0,
        tiled=True,
    ).reshape(2, slots, 2 * width)
    far = ring_size // 2
    held = {(0, 0, 0): own, (0, 1, 0): swapped(own)}
    raw = {}
    for step in range(1, far + 1):
        for chain in range(2 if step < far else 1):
            piece = lax.ppermute(held[step - 1, chain, 0], ("ring", "core"), around)
            raw[step, chain, 0] = piece
            if step > 1:
                crossed = swapped(held[step - 1, chain, 0])
                raw[step - 1, chain, 1] = crossed
                piece, crossed = lax.optimization_barrier((piece, crossed))
                held[step - 1, chain, 1] = crossed
            held[step, chain, 0] = piece
    held[far - 1, 1, 1] = swapped(held[far - 1, 1, 0])
    held[far, 0, 1] = swapped(held[far, 0, 0])
    blocks = list(held)
    index = jnp.stack([lax.axis_index("ring"), lax.axis_index("core")]).astype(jnp.int32)
    hidden_units = expert_weights.shape[2]
    features = expert_weights.shape[3]
    vmem_spec = pl.BlockSpec(memory_space=pltpu.VMEM)
    smem_spec = pl.BlockSpec(memory_space=pltpu.SMEM)
    piece_bytes = 8 * slots * width
    weight_bytes = 6 * hidden_units * features
    block_flops = 12 * slots * width * hidden_units
    early = {
        "early_0": [(0, 0, 0), (0, 1, 0)],
        "early_1": [(1, c, t) for t in range(2) for c in range(2)],
        "early_2": [(s, c, t) for s in range(2, far - 1) for t in range(2) for c in range(2)],
        "early_3": [(far - 1, 0, 0), (far - 1, 0, 1), (far - 1, 1, 0)],
        "early_4": [(far - 1, 1, 1), (far, 0, 0)],
    }
    late = [(far, 0, 1)]
    from_hbm = [(1, 1, 0), (1, 0, 1), (2, 0, 0)]
    sums = jax.ShapeDtypeStruct((3 * hidden_units, slots), F32)

    partials = []
    for chosen in early.values():
        chained = len(partials)
        partials = [
            pl.pallas_call(
                functools.partial(forward_kernel, ring_size, chosen, chained),
                out_shape=sums,
                in_specs=[smem_spec, vmem_spec] + [vmem_spec] * (chained + len(chosen)),
                out_specs=pl.BlockSpec(memory_space=pltpu.VMEM),
                cost_estimate=pl.CostEstimate(
                    flops=len(chosen) * block_flops,
                    bytes_accessed=len(chosen) * piece_bytes,
                    transcendentals=0,
                ),
                compiler_params=pltpu.CompilerParams(vmem_limit_bytes=EARLY_VMEM),
            )(index, expert_weights, *partials, *[raw.get(k, held[k]) for k in chosen])
        ]
    return pl.pallas_call(
        functools.partial(grads_kernel, ring_size, blocks, late, from_hbm),
        out_shape=jax.ShapeDtypeStruct(expert_weights.shape, BF16),
        in_specs=[smem_spec, vmem_spec, vmem_spec]
        + [pl.BlockSpec(memory_space=pl.ANY) if k in from_hbm else vmem_spec for k in blocks],
        out_specs=pl.BlockSpec(memory_space=pl.ANY),
        scratch_shapes=[
            pltpu.VMEM(sums.shape, F32),
            pltpu.VMEM((len(blocks), 2, 3, hidden_units, width), BF16),
            pltpu.SemaphoreType.DMA((len(blocks), 2)),
            pltpu.VMEM((len(from_hbm), 2, slots, 2 * width), BF16),
            pltpu.SemaphoreType.DMA((len(from_hbm),)),
        ],
        cost_estimate=pl.CostEstimate(
            flops=len(blocks) * block_flops,
            bytes_accessed=len(blocks) * piece_bytes + weight_bytes,
            transcendentals=slots * hidden_units,
        ),
        compiler_params=pltpu.CompilerParams(vmem_limit_bytes=GRADS_VMEM),
    )(index, expert_weights, *partials, *[held[k] for k in blocks])


def solution(mesh):
    sizes = dict(zip(mesh.axis_names, mesh.devices.shape))
    fine = Mesh(
        mesh.devices.reshape(2, sizes["dp"] // 4, 2, sizes["expert"]),
        ("half", "ring", "core", "expert"),
    )
    dp = ("half", "ring", "core")
    return jax.shard_map(
        device_step,
        mesh=fine,
        in_specs=(
            P("expert", dp),
            P("expert", dp),
            P("expert", None),
            P("expert", None),
            P("expert", None, dp, None),
        ),
        out_specs=P("expert", None, dp, None),
        check_vma=False,
    )
```

```python
import functools

import jax
import jax.numpy as jnp
from jax import lax
from jax.experimental import pallas as pl
from jax.experimental.pallas import tpu as pltpu
from jax.sharding import Mesh
from jax.sharding import PartitionSpec as P

CAP = 40
BF16 = jnp.bfloat16
F32 = jnp.float32
EARLY_VMEM = 8 << 20
GRADS_VMEM = 16 << 20
FORWARD_GROUP = 2
GRADS_GROUP = 4


def pack_kernel(routes_ref, gates_ref, tokens_ref, cotangent_ref, out_ref):
    tokens = routes_ref.shape[1]
    copies, slots, width = out_ref.shape
    experts = slots // CAP
    ids = lax.broadcasted_iota(jnp.int32, (experts, tokens), 0)
    named = jnp.zeros((experts, tokens), F32)
    weight = jnp.zeros((experts, tokens), F32)
    for k in range(routes_ref.shape[0]):
        hit = routes_ref[k : k + 1, :] == ids
        named = named + jnp.where(hit, 1.0, 0.0)
        weight = weight + jnp.where(hit, gates_ref[k : k + 1, :], 0.0)
    down = lax.broadcasted_iota(jnp.int32, (tokens, tokens), 0)
    across = lax.broadcasted_iota(jnp.int32, (tokens, tokens), 1)
    before = jnp.where(down < across, 1.0, 0.0).astype(BF16)
    earlier = jnp.dot(named.astype(BF16), before, preferred_element_type=F32)
    place = jnp.where(named > 0.0, earlier, -1.0)
    places = lax.broadcasted_iota(jnp.int32, (CAP, tokens), 0).astype(F32)
    select, weights = [], []
    for e in range(experts):
        hit = place[e : e + 1, :] == places
        select.append(jnp.where(hit, 1.0, 0.0))
        weights.append(jnp.sum(jnp.where(hit, weight[e : e + 1, :], 0.0), axis=1, keepdims=True))
    select = jnp.concatenate(select, axis=0).astype(BF16)
    weights = jnp.concatenate(weights, axis=0)
    rows = jnp.dot(select, tokens_ref[...], preferred_element_type=F32).astype(BF16)
    scaled = jnp.dot(select, cotangent_ref[...], preferred_element_type=F32)
    scaled = (scaled * weights).astype(BF16)
    for j in range(copies):
        out_ref[j, :, : width // 2] = rows
        out_ref[j, :, width // 2 :] = scaled


def column(index_ref, ring_size, half, block, j):
    step, chain, turned = block
    ring, core = index_ref[0], index_ref[1]
    way = (1 - 2 * core) * (1 - 2 * turned)
    z = lax.rem(ring - way * step + 2 * ring_size, ring_size)
    other = chain ^ turned
    c = core + other - 2 * core * other
    return pl.multiple_of(((j * ring_size + z) * 2 + c) * half, half)


def joined(pieces, part):
    half = pieces[0].shape[2] // 2
    cut = slice(part * half, (part + 1) * half)
    return jnp.concatenate(
        [piece[j, :, cut] for piece in pieces for j in range(piece.shape[0])], axis=1
    )


def add_forward(ring_size, index_ref, weights_ref, total, pieces, blocks):
    halves, half = pieces[0].shape[0], pieces[0].shape[2] // 2
    hidden_units = weights_ref.shape[2]
    along = (((1,), (1,)), ((), ()))

    def weight_block(m):
        return jnp.concatenate(
            [
                weights_ref[0, m, :, pl.ds(column(index_ref, ring_size, half, block, j), half)]
                for block in blocks
                for j in range(halves)
            ],
            axis=1,
        )

    pair = jnp.concatenate([weight_block(0), weight_block(1)], axis=0)
    total[: 2 * hidden_units] += lax.dot_general(
        pair, joined(pieces, 0), along, preferred_element_type=F32
    )
    total[2 * hidden_units :] += lax.dot_general(
        weight_block(2), joined(pieces, 1), along, preferred_element_type=F32
    )


def forward_kernel(ring_size, blocks, chained, index_ref, weights_ref, *refs):
    count = len(blocks)
    partials, sources, total = refs[:chained], refs[chained : chained + count], refs[chained + count]
    total[...] = partials[0][...] if chained else jnp.zeros_like(total)
    for k in range(0, count, FORWARD_GROUP):
        chosen = range(k, min(k + FORWARD_GROUP, count))
        add_forward(
            ring_size, index_ref, weights_ref, total,
            [sources[n] for n in chosen], [blocks[n] for n in chosen],
        )


def grads_kernel(ring_size, blocks, late, index_ref, weights_ref, partial_ref, *refs):
    count = len(blocks)
    sources, out_ref = refs[:count], refs[count]
    total, out_buf, sems = refs[count + 1 :]
    halves, half = sources[0].shape[0], sources[0].shape[2] // 2
    hidden_units = weights_ref.shape[2]
    last = [blocks.index(block) for block in late]
    total[...] = partial_ref[...]
    add_forward(ring_size, index_ref, weights_ref, total, [sources[k] for k in last], late)
    gate_part = total[:hidden_units]
    up_part = total[hidden_units : 2 * hidden_units]
    back_hidden = total[2 * hidden_units :]
    sigmoid_part = jax.nn.sigmoid(gate_part)
    silu = gate_part * sigmoid_part
    hidden = (silu * up_part).astype(BF16)
    derivative = sigmoid_part * (1.0 + gate_part * (1.0 - sigmoid_part))
    pre_gate = (back_hidden * up_part * derivative).astype(BF16)
    pre_up = (back_hidden * silu).astype(BF16)
    both = jnp.concatenate([pre_gate, pre_up], axis=0)
    copies = []
    for n in range(0, count, GRADS_GROUP):
        chosen = range(n, min(n + GRADS_GROUP, count))
        pieces = [sources[k] for k in chosen]
        ins = jnp.dot(both, joined(pieces, 0), preferred_element_type=F32).astype(BF16)
        outs = jnp.dot(hidden, joined(pieces, 1), preferred_element_type=F32).astype(BF16)
        for m, k in enumerate(chosen):
            for j in range(halves):
                cut = slice((m * halves + j) * half, (m * halves + j + 1) * half)
                out_buf[k, j, 0] = ins[:hidden_units, cut]
                out_buf[k, j, 1] = ins[hidden_units:, cut]
                out_buf[k, j, 2] = outs[:, cut]
                cols = pl.ds(column(index_ref, ring_size, half, blocks[k], j), half)
                copy = pltpu.make_async_copy(
                    out_buf.at[k, j], out_ref.at[0, :, :, cols], sems.at[k, j]
                )
                copy.start()
                copies.append(copy)
    for copy in copies:
        copy.wait()


def device_step(tokens, cotangent, routes, gates, expert_weights):
    groups = lax.axis_size("expert")
    ring_size = lax.axis_size("ring")
    slots = groups * CAP
    width = tokens.shape[1]
    send = pl.pallas_call(
        pack_kernel,
        out_shape=jax.ShapeDtypeStruct((2, slots, 2 * width), BF16),
    )(routes.T, gates.T, tokens, cotangent)
    around = [
        (z * 2 + c, ((z + 1 - 2 * c) % ring_size) * 2 + c)
        for z in range(ring_size)
        for c in range(2)
    ]

    def swapped(x):
        return lax.ppermute(x, "core", [(0, 1), (1, 0)])

    own = lax.all_to_all(
        send.reshape(2 * groups, CAP, 2 * width),
        ("half", "expert"),
        split_axis=0,
        concat_axis=0,
        tiled=True,
    ).reshape(2, slots, 2 * width)
    far = ring_size // 2
    held = {(0, 0, 0): own, (0, 1, 0): swapped(own)}
    raw = {}
    for step in range(1, far + 1):
        for chain in range(2 if step < far else 1):
            piece = lax.ppermute(held[step - 1, chain, 0], ("ring", "core"), around)
            raw[step, chain, 0] = piece
            if step > 1:
                crossed = swapped(held[step - 1, chain, 0])
                raw[step - 1, chain, 1] = crossed
                piece, crossed = lax.optimization_barrier((piece, crossed))
                held[step - 1, chain, 1] = crossed
            held[step, chain, 0] = piece
    held[far - 1, 1, 1] = swapped(held[far - 1, 1, 0])
    held[far, 0, 1] = swapped(held[far, 0, 0])
    blocks = list(held)
    index = jnp.stack([lax.axis_index("ring"), lax.axis_index("core")]).astype(jnp.int32)
    hidden_units = expert_weights.shape[2]
    features = expert_weights.shape[3]
    vmem_spec = pl.BlockSpec(memory_space=pltpu.VMEM)
    smem_spec = pl.BlockSpec(memory_space=pltpu.SMEM)
    piece_bytes = 8 * slots * width
    weight_bytes = 6 * hidden_units * features
    block_flops = 12 * slots * width * hidden_units
    early = {
        "early_0": [(0, 0, 0), (0, 1, 0)],
        "early_1": [(1, c, t) for t in range(2) for c in range(2)],
        "early_2": [(s, c, t) for s in range(2, far - 1) for t in range(2) for c in range(2)],
        "early_3": [(far - 1, 0, 0), (far - 1, 0, 1), (far - 1, 1, 0)],
        "early_4": [(far - 1, 1, 1), (far, 0, 0)],
    }
    late = [(far, 0, 1)]
    sums = jax.ShapeDtypeStruct((3 * hidden_units, slots), F32)

    partials = []
    for chosen in early.values():
        chained = len(partials)
        partials = [
            pl.pallas_call(
                functools.partial(forward_kernel, ring_size, chosen, chained),
                out_shape=sums,
                in_specs=[smem_spec, vmem_spec] + [vmem_spec] * (chained + len(chosen)),
                out_specs=pl.BlockSpec(memory_space=pltpu.VMEM),
                cost_estimate=pl.CostEstimate(
                    flops=len(chosen) * block_flops,
                    bytes_accessed=len(chosen) * piece_bytes,
                    transcendentals=0,
                ),
                compiler_params=pltpu.CompilerParams(vmem_limit_bytes=EARLY_VMEM),
            )(index, expert_weights, *partials, *[raw.get(k, held[k]) for k in chosen])
        ]
    return pl.pallas_call(
        functools.partial(grads_kernel, ring_size, blocks, late),
        out_shape=jax.ShapeDtypeStruct(expert_weights.shape, BF16),
        in_specs=[smem_spec, vmem_spec, vmem_spec] + [vmem_spec] * len(blocks),
        out_specs=pl.BlockSpec(memory_space=pl.ANY),
        scratch_shapes=[
            pltpu.VMEM(sums.shape, F32),
            pltpu.VMEM((len(blocks), 2, 3, hidden_units, width), BF16),
            pltpu.SemaphoreType.DMA((len(blocks), 2)),
        ],
        cost_estimate=pl.CostEstimate(
            flops=len(blocks) * block_flops,
            bytes_accessed=len(blocks) * piece_bytes + weight_bytes,
            transcendentals=slots * hidden_units,
        ),
        compiler_params=pltpu.CompilerParams(vmem_limit_bytes=GRADS_VMEM),
    )(index, expert_weights, *partials, *[held[k] for k in blocks])


def solution(mesh):
    sizes = dict(zip(mesh.axis_names, mesh.devices.shape))
    fine = Mesh(
        mesh.devices.reshape(2, sizes["dp"] // 4, 2, sizes["expert"]),
        ("half", "ring", "core", "expert"),
    )
    dp = ("half", "ring", "core")
    return jax.shard_map(
        device_step,
        mesh=fine,
        in_specs=(
            P("expert", dp),
            P("expert", dp),
            P("expert", None),
            P("expert", None),
            P("expert", None, dp, None),
        ),
        out_specs=P("expert", None, dp, None),
        check_vma=False,
    )
```
